128 devices in a mesh: mod: 16 (over x, y_hi, core), sp: 8 (over y_lo, z).
Axes of the slice: x: 4, y: 4 (y_hi: 2, y_lo: 2; y = y_hi * 2 + y_lo), z: 4, core: 2. Of those that a mesh axis runs over, the one named last changes fastest.
Arguments:
- images: bfloat16 [16, 512, 64, 256], P('mod', None, 'sp'), may hold values from -6 to 6
- conv_first: bfloat16 [16, 256, 256], P('mod'), may hold values from -0.375 to 0.375
- conv_second: bfloat16 [16, 4096, 256], P('mod'), may hold values from -0.09375 to 0.09375
- project: bfloat16 [16, 256, 512], P('mod'), may hold values from -0.375 to 0.375
- whiten: bfloat16 [16, 512, 256], P('mod'), may hold values from -0.25 to 0.25
- valid_mask: int32 [16, 512, 16, 4], P('mod', None, 'sp'), may hold values 0 or 1
- scene_index: int32 [512], replicated, may hold values from 0 to 63
Outputs:
- target: float32 [512, 256], P('sp')
- grad_view: bfloat16 [16, 512, 256], P('mod', 'sp')
- grad_whiten: float32 [16, 512, 256], P('mod', 'sp')
The draws below stay inside these ranges and needn't reach their ends.
Inputs may be any that keep to these rules, and one draw needn't show every extreme that they name: `valid_mask`: 1 where a pixel of the encoded map is cloud-free.
All inputs are finite; a program needn't handle non-finite values. No bound on the sum of `valid_mask` on one device may be relied on, other than what follows from the above.
Results may differ from the reference program's by a relative error of at most 0.028.
Values may be sent and summed in bfloat16 or wider, within the bound.
No kernel may reach another device: no remote copies, remote signals or barrier semaphores. Data moves between devices by JAX's collectives and lax.ppermute only.
A program may use at most 192 MiB of HBM per device.

```python
import math
import jax
import jax.numpy as jnp
import numpy as np
from jax import lax

BANDS = 16
CH = 256
F = 512
K = 256
SCENES = 64
SAMPLES = 512
COLS = 16
ROWS = 64
MODS = 16


def place_ends(result, stream_key, low, high):
    extent = result.shape
    spot = [jax.random.randint(jax.random.fold_in(stream_key, axis), (), 0, extent[axis]) for axis in range(len(extent))]
    result = result.at[tuple(spot)].set(low)
    longest = extent.index(max(extent))
    spot[longest] = (spot[longest] + 1) % extent[longest]
    return result.at[tuple(spot)].set(high)


def block_levels(stream_key, shape, shards, low, top_value):
    gain, own = 1.0, jax.random.fold_in(stream_key, 6)
    for position, shards_of in shards:
        draws = jnp.exp(jax.random.uniform(jax.random.fold_in(own, position), (shards_of,), jnp.float32, low / len(shards), top_value / len(shards)))
        gain = gain * jnp.repeat(draws, shape[position] // shards_of).reshape([-1 if axis == position else 1 for axis in range(len(shape))])
    return gain


def cumulative_ranks(count, skew):
    portions = [(1 << 20) // math.isqrt(standing ** skew) + 1 for standing in range(1, count + 1)]
    width = 1 + sum(portions) // (1 << 30)
    return np.cumsum(np.array([max(1, weight // width) for weight in portions]))


def ranked(key, shape, amount, slope):
    grid = cumulative_ranks(amount, slope)
    lot = jax.random.randint(jax.random.fold_in(key, 1), shape, 0, int(grid[amount - 1]))
    standing = jnp.searchsorted(jnp.asarray(grid, jnp.int32), lot, side="right")
    return jax.random.permutation(jax.random.fold_in(key, 2), amount)[standing].astype(jnp.int32)


def centred(key, dims, deviation, limit, split=(), held_as=jnp.bfloat16):
    array = deviation * jax.random.normal(key, dims, jnp.float32)
    if split:
        array = array * block_levels(key, dims, split, -0.22, 0.18)
    return jnp.clip(array, -limit, limit).astype(held_as)


def setup_inputs(seed: int = 0) -> dict:
    splits = jax.random.split(jax.random.key(seed), 8)
    images = centred(splits[0], (MODS, SAMPLES, ROWS, COLS * BANDS), 1.0, 6.0, ((0, 16), (2, 8)))
    conv_first = centred(splits[1], (MODS, 16 * BANDS, CH), (16 * BANDS) ** -0.5, 0.375, ((0, 16),))
    conv_second = centred(splits[2], (MODS, 16 * CH, CH), (16 * CH) ** -0.5, 0.09375, ((0, 16),))
    project = centred(splits[3], (MODS, CH, F), CH ** -0.5, 0.375, ((0, 16),))
    whiten = centred(splits[4], (MODS, F, K), F ** -0.5, 0.25, ((0, 16),))
    valid_mask = place_ends((jax.random.randint(splits[5], (MODS, SAMPLES, ROWS // 4, COLS // 4), 0, 4) < 3).astype(jnp.int32), jax.random.fold_in(splits[5], 1), 0, 1)
    scene_index = place_ends(ranked(splits[6], (SAMPLES,), SCENES, 4), jax.random.fold_in(splits[6], 3), 0, SCENES - 1).astype(jnp.int32)
    return dict(images=images, conv_first=conv_first, conv_second=conv_second, project=project, whiten=whiten, valid_mask=valid_mask, scene_index=scene_index)


def stride_conv(padded, weight, depth, per_tap):
    count, rows_in, wide = padded.shape
    columns = wide // depth
    sided = jnp.pad(padded, ((0, 0), (0, 0), (depth, depth)))
    paired = sided.reshape(count, rows_in, columns // 2 + 1, 2 * depth)
    joined = jnp.concatenate([paired[:, :, :-1], paired[:, :, 1:]], axis=-1)
    rows_out = (rows_in - 2) // 2
    span = 4 * depth
    taps = [joined[:, offset:offset + 2 * rows_out:2] for offset in range(4)]
    if per_tap:
        total = jnp.zeros((count * rows_out * (columns // 2), weight.shape[1]), jnp.float32)
        for offset in range(4):
            total = total + jnp.dot(taps[offset].reshape(-1, span).astype(jnp.float32), weight[offset * span:(offset + 1) * span].astype(jnp.float32), preferred_element_type=jnp.float32)
    else:
        total = jnp.dot(jnp.concatenate(taps, axis=-1).reshape(-1, 4 * span).astype(jnp.float32), weight.astype(jnp.float32), preferred_element_type=jnp.float32)
    return jnp.maximum(total, 0.0).astype(jnp.bfloat16).reshape(count, rows_out, columns // 2 * weight.shape[1])

def reference(images, conv_first, conv_second, project, whiten, valid_mask, scene_index):

    def encode(parts):
        image, first_w, second_w, mask = parts
        padded = jnp.pad(image, ((0, 0), (1, 1), (0, 0)))
        first = stride_conv(padded, first_w, BANDS, False)
        second = stride_conv(jnp.pad(first, ((0, 0), (1, 1), (0, 0))), second_w, CH, True)
        pixels = second.reshape(second.shape[0], -1, CH).astype(jnp.float32)
        weights = mask.reshape(mask.shape[0], -1).astype(jnp.float32)
        return jnp.einsum('npc,np->nc', pixels, weights) / pixels.shape[1]
    pooled = lax.map(encode, (images, conv_first, conv_second, valid_mask))
    onehot = (scene_index[:, None] == jnp.arange(SCENES, dtype=jnp.int32)[None, :]).astype(jnp.float32)
    counts = lax.optimization_barrier(jnp.sum(onehot, axis=0))

    def view_of(parts):
        pooled_m, project_m, whiten_m = parts
        feat = jnp.dot(pooled_m.astype(jnp.bfloat16).astype(jnp.float32), project_m.astype(jnp.float32), preferred_element_type=jnp.float32)
        sums = jnp.dot(onehot.T, feat, precision=lax.Precision.HIGHEST)
        means = sums / jnp.maximum(counts, 1.0)[:, None]
        panel = (feat - jnp.dot(onehot, means, precision=lax.Precision.HIGHEST)).astype(jnp.bfloat16)
        raw = jnp.dot(panel.astype(jnp.float32), whiten_m.astype(jnp.float32), preferred_element_type=jnp.float32)
        scale = 1.0 / jnp.sqrt(lax.optimization_barrier(jnp.mean(raw * raw, axis=-1, keepdims=True)) + 1e-05)
        view = (raw * scale).astype(jnp.bfloat16)
        return (panel, scale, view)
    panels, scales, views = lax.map(view_of, (pooled, project, whiten))
    views_f = views.astype(jnp.float32)
    eye = jnp.eye(K, dtype=jnp.float32)
    mean_view = lax.optimization_barrier(jnp.sum(views_f, axis=0)) / MODS
    gram = jnp.dot(mean_view.T, mean_view, precision=lax.Precision.HIGHEST) / SAMPLES + 0.001 * eye
    lower = jnp.linalg.cholesky(gram)
    target = jax.scipy.linalg.solve_triangular(lower, mean_view.T, lower=True).T

    def grads_of(parts):
        panel, scale, view_f = parts
        blocks = jnp.einsum('nk,mnl->mkl', view_f, views_f, precision=lax.Precision.HIGHEST) / SAMPLES
        coupling = jnp.einsum('mnl,mkl->nk', views_f, blocks - eye, precision=lax.Precision.HIGHEST)
        grad_full = view_f - target + coupling
        inner = lax.optimization_barrier(jnp.mean(grad_full * view_f, axis=-1, keepdims=True))
        grad_raw = ((grad_full - view_f * inner) * scale).astype(jnp.bfloat16)
        grad_w = jnp.dot(panel.T.astype(jnp.float32), grad_raw.astype(jnp.float32), preferred_element_type=jnp.float32)
        return (grad_full.astype(jnp.bfloat16), grad_w)
    grad_view, grad_whiten = lax.map(grads_of, (panels, scales, views_f))
    return (target, grad_view, grad_whiten)
```

```python
import jax
import jax.numpy as jnp
from jax import lax
from jax.experimental import pallas as pl
from jax.experimental.pallas import tpu as pltpu
from jax.sharding import PartitionSpec as P

BANDS = 16
CH = 256
SCENES = 64
HALO = 3


def conv_kernel(edge_ref, x_ref, up_ref, dn_ref, w1_ref, w2_ref, mask_ref, out_ref, band_ref, first_ref):
    samples = x_ref.shape[1]
    rows = x_ref.shape[0]
    cells = mask_ref.shape[1]
    window = 4 * BANDS
    groups = ((0, (0, 1, 2)), (64, (3, 4)), (128, (5, 6, 7)))
    band_ref[...] = jnp.zeros_like(band_ref)
    for start, columns in groups:
        for column in columns:
            low = 2 * BANDS * column - BANDS
            begin, end = (max(low, 0), min(low + window, 256))
            for tap in range(4):
                band_ref[
                    tap * 128 + begin - start : tap * 128 + end - start,
                    column * CH : (column + 1) * CH,
                ] = w1_ref[tap * window + begin - low : tap * window + end - low, :]

    def image_row(row):
        if row < 0:
            return up_ref.at[row + HALO]
        if row >= rows:
            return dn_ref.at[row - rows]
        return x_ref.at[row]

    out_rows = rows // 2
    for row in range(-1, out_rows + 1):
        taps = [image_row(2 * row + tap - 1) for tap in range(4)]
        for start, columns in groups:
            left = jnp.concatenate([tap[:, start : start + 128] for tap in taps], axis=1)
            lanes = slice(columns[0] * CH, (columns[-1] + 1) * CH)
            total = jnp.dot(left, band_ref[:, lanes], preferred_element_type=jnp.float32)
            total = jnp.maximum(total, 0.0)
            if row == -1:
                total = total * edge_ref[0]
            if row == out_rows:
                total = total * edge_ref[1]
            first_ref[row + 1, :, lanes] = total.astype(jnp.bfloat16)
    pooled = jnp.zeros((samples, CH), jnp.float32)
    for row in range(out_rows // 2):
        for column in range(4):
            low, high = (max(2 * column - 1, 0), min(2 * column + 3, 8))
            skip = low - (2 * column - 1)
            total = None
            for tap in range(4):
                part = jnp.dot(
                    first_ref[2 * row + tap, :, low * CH : high * CH],
                    w2_ref[(tap * 4 + skip) * CH : (tap * 4 + skip + high - low) * CH, :],
                    preferred_element_type=jnp.float32,
                )
                total = part if total is None else total + part
            pixel = jnp.maximum(total, 0.0).astype(jnp.bfloat16).astype(jnp.float32)
            cell = row * 4 + column
            pooled = pooled + pixel * mask_ref[:, cell : cell + 1]
    out_ref[...] = pooled


def encode(edge, x, up, dn, w1, w2, mask):
    samples = x.shape[1]
    vmem = pl.BlockSpec(memory_space=pltpu.VMEM)
    return pl.pallas_call(
        conv_kernel,
        out_shape=jax.ShapeDtypeStruct((samples, CH), jnp.float32),
        in_specs=[pl.BlockSpec(memory_space=pltpu.SMEM)] + [vmem] * 6,
        out_specs=vmem,
        scratch_shapes=[
            pltpu.VMEM((512, 8 * CH), jnp.bfloat16),
            pltpu.VMEM((x.shape[0] // 2 + 2, samples, 8 * CH), jnp.bfloat16),
        ],
        compiler_params=pltpu.CompilerParams(vmem_limit_bytes=56 * 1024 * 1024),
        name="encode",
    )(edge, x, up, dn, w1, w2, mask)


def swap(x, axis):
    return lax.all_to_all(x, axis, 0, 0, tiled=True)


def spread(x, axis):
    return swap(jnp.broadcast_to(x[None], (lax.axis_size(axis),) + x.shape), axis)


def on_device(images, conv_first, conv_second, project, whiten, valid_mask, scene_index):
    samples = images.shape[1]
    size = lax.axis_size("sp")
    mods = lax.axis_size("mod")
    place = lax.axis_index("sp")
    share = samples // size
    first_row = place * share
    x = jnp.transpose(images[0], (1, 0, 2))
    up = [(i, i + 1) for i in range(size - 1)]
    down = [(j, i) for i, j in up]
    before = lax.ppermute(x[x.shape[0] - HALO :], "sp", up)
    after = lax.ppermute(x[:HALO], "sp", down)
    edge = jnp.stack([place > 0, place < size - 1]).astype(jnp.float32)
    mask_rows = valid_mask[0].reshape(samples, -1).astype(jnp.float32)
    cells = mask_rows.shape[1] * size
    part = encode(edge, x, before, after, conv_first[0], conv_second[0], mask_rows)
    pieces = swap(part.reshape(size, share, CH), "sp")
    pooled_rows = (jnp.sum(pieces, axis=0) / cells).astype(jnp.bfloat16)
    pooled = spread(pooled_rows, "sp").reshape(samples, CH)

    onehot = (scene_index[:, None] == jnp.arange(SCENES, dtype=jnp.int32)[None, :]).astype(
        jnp.float32
    )
    counts = jnp.sum(onehot, axis=0)
    feat = jnp.dot(pooled, project[0], preferred_element_type=jnp.float32)
    sums = jnp.dot(onehot.T, feat, precision=lax.Precision.HIGHEST)
    means = sums / jnp.maximum(counts, 1.0)[:, None]
    panel = (feat - jnp.dot(onehot, means, precision=lax.Precision.HIGHEST)).astype(jnp.bfloat16)
    raw = jnp.dot(panel, whiten[0], preferred_element_type=jnp.float32)
    scale = 1.0 / jnp.sqrt(jnp.mean(raw * raw, axis=-1, keepdims=True) + 1e-05)
    view = (raw * scale).astype(jnp.bfloat16)

    view_rows = lax.dynamic_slice_in_dim(view, first_row, share, 0)
    scale_rows = lax.dynamic_slice_in_dim(scale, first_row, share, 0)
    inner_part = lax.dot_general(
        view_rows, view, (((1,), (1,)), ((), ())), preferred_element_type=jnp.float32
    )
    inner_pieces = swap(inner_part.reshape(mods, share // mods, samples), "mod")
    view_pieces = swap(view.reshape(mods, samples // mods, CH), "mod")
    inner_sum = jnp.sum(inner_pieces, axis=0)
    view_sum = jnp.sum(view_pieces.astype(jnp.float32), axis=0)
    inner_rows = spread(inner_sum, "mod").reshape(share, samples)
    total = spread(view_sum, "mod").reshape(samples, CH)

    eye = jnp.eye(CH, dtype=jnp.float32)
    mean_view = total / mods
    gram = jnp.dot(mean_view.T, mean_view, precision=lax.Precision.HIGHEST) / samples + 0.001 * eye
    lower = jnp.linalg.cholesky(gram)
    total_rows = lax.dynamic_slice_in_dim(total, first_row, share, 0)
    mean_rows = total_rows / mods
    target_rows = jax.scipy.linalg.solve_triangular(lower, mean_rows.T, lower=True).T
    view_f = view_rows.astype(jnp.float32)
    coupling = (
        jnp.dot(inner_rows, view.astype(jnp.float32), precision=lax.Precision.HIGHEST) / samples
        - total_rows
    )
    grad_full = view_f - target_rows + coupling
    inner = jnp.mean(grad_full * view_f, axis=-1, keepdims=True)
    grad_raw = ((grad_full - view_f * inner) * scale_rows).astype(jnp.bfloat16)
    grad_raw_all = spread(grad_raw, "sp").reshape(samples, CH)
    wide = whiten.shape[1] // size
    panel_own = lax.dynamic_slice_in_dim(panel, place * wide, wide, 1)
    grad_w = lax.dot_general(
        panel_own, grad_raw_all, (((0,), (0,)), ((), ())), preferred_element_type=jnp.float32
    )
    return (target_rows, grad_full.astype(jnp.bfloat16)[None], grad_w[None])


def solution(mesh):
    placed = (
        P("mod", None, "sp", None),
        P("mod", None, None),
        P("mod", None, None),
        P("mod", None, None),
        P("mod", None, None),
        P("mod", None, "sp", None),
        P(),
    )
    return jax.shard_map(
        on_device,
        mesh=mesh,
        in_specs=placed,
        out_specs=(P("sp", None), P("mod", "sp", None), P("mod", "sp", None)),
        check_vma=False,
    )
```

```python
import jax
import jax.numpy as jnp
from jax import lax
from jax.experimental import pallas as pl
from jax.experimental.pallas import tpu as pltpu
from jax.sharding import PartitionSpec as P

BANDS = 16
CH = 256
SCENES = 64
EXTRA = 8


def conv_kernel(got_ref, w1_ref, w2_ref, out_ref, padded_ref, band_ref, first_ref):
    sources = got_ref.shape[0]
    share = out_ref.shape[0]
    rows = (got_ref.shape[1] - EXTRA) // share
    window = 4 * BANDS
    groups = ((0, (0, 1, 2)), (64, (3, 4)), (128, (5, 6, 7)))
    band_ref[...] = jnp.zeros_like(band_ref)
    for start, columns in groups:
        for column in columns:
            low = 2 * BANDS * column - BANDS
            begin, end = (max(low, 0), min(low + window, 256))
            for tap in range(4):
                band_ref[
                    tap * 128 + begin - start : tap * 128 + end - start,
                    column * CH : (column + 1) * CH,
                ] = w1_ref[tap * window + begin - low : tap * window + end - low, :]

    total_rows = sources * rows
    blank = jnp.zeros((share, 256), jnp.bfloat16)
    padded_ref[0, 0] = blank
    padded_ref[total_rows // 2, 1] = blank
    for source in range(sources):
        for row in range(rows):
            place = source * rows + row + 1
            padded_ref[place // 2, place % 2] = got_ref[source, row * share : (row + 1) * share, :]
    blank = jnp.zeros((share, 8 * CH), jnp.bfloat16)
    first_ref[0, 0] = blank
    first_ref[total_rows // 4, 1] = blank

    def first_rows(group, carry):
        for start, columns in groups:
            left = jnp.concatenate(
                [
                    padded_ref[
                        pl.ds(group * 8 + tap // 2, 8), tap % 2, :, start : start + 128
                    ].reshape(8 * share, 128)
                    for tap in range(4)
                ],
                axis=1,
            )
            lanes = slice(columns[0] * CH, (columns[-1] + 1) * CH)
            total = jnp.dot(left, band_ref[:, lanes], preferred_element_type=jnp.float32)
            total = jnp.maximum(total, 0.0).astype(jnp.bfloat16)
            for row in range(8):
                first_ref[group * 4 + (row + 1) // 2, (row + 1) % 2, :, lanes] = total[
                    row * share : (row + 1) * share
                ]
        return carry

    lax.fori_loop(0, total_rows // 16, first_rows, 0)

    span = 8 * share
    spot = lax.broadcasted_iota(jnp.int32, (share, span), 1) % share
    mine = spot == lax.broadcasted_iota(jnp.int32, (share, span), 0)
    pooled = jnp.zeros((share, CH), jnp.float32)
    for group in range(total_rows // 32):
        for column in range(4):
            low, high = (max(2 * column - 1, 0), min(2 * column + 3, 8))
            skip = low - (2 * column - 1)
            total = None
            for tap in range(4):
                left = first_ref[
                    group * 8 + tap // 2 : group * 8 + tap // 2 + 8, tap % 2, :, low * CH : high * CH
                ]
                part = jnp.dot(
                    left.reshape(span, (high - low) * CH),
                    w2_ref[(tap * 4 + skip) * CH : (tap * 4 + skip + high - low) * CH, :],
                    preferred_element_type=jnp.float32,
                )
                total = part if total is None else total + part
            pixel = jnp.maximum(total, 0.0).astype(jnp.bfloat16)
            row = rows * share + column
            valid = jnp.concatenate(
                [
                    got_ref[group * 4 + source, row : row + 1, : 2 * share].astype(jnp.float32)
                    for source in range(4)
                ],
                axis=1,
            )
            chosen = jnp.where(mine, valid, 0.0).astype(jnp.bfloat16)
            pooled = pooled + jnp.dot(chosen, pixel, preferred_element_type=jnp.float32)
    cells = total_rows
    out_ref[...] = (pooled / cells).astype(jnp.bfloat16)


def encode(got, w1, w2, share):
    rows = got.shape[0] * (got.shape[1] - EXTRA) // share
    vmem = pl.BlockSpec(memory_space=pltpu.VMEM)
    return pl.pallas_call(
        conv_kernel,
        out_shape=jax.ShapeDtypeStruct((share, CH), jnp.bfloat16),
        in_specs=[vmem] * 3,
        out_specs=vmem,
        scratch_shapes=[
            pltpu.VMEM((rows // 2 + 1, 2, share, 256), jnp.bfloat16),
            pltpu.VMEM((512, 8 * CH), jnp.bfloat16),
            pltpu.VMEM((rows // 4 + 1, 2, share, 8 * CH), jnp.bfloat16),
        ],
        compiler_params=pltpu.CompilerParams(vmem_limit_bytes=56 * 1024 * 1024),
        name="encode",
    )(got, w1, w2)


def swap(x, axis):
    return lax.all_to_all(x, axis, 0, 0, tiled=True)


def spread(x, axis):
    return swap(jnp.broadcast_to(x[None], (lax.axis_size(axis),) + x.shape), axis)


def on_device(images, conv_first, conv_second, project, whiten, valid_mask, scene_index):
    samples = images.shape[1]
    size = lax.axis_size("sp")
    mods = lax.axis_size("mod")
    place = lax.axis_index("sp")
    share = samples // size
    first_row = place * share
    rows = images.shape[2]
    x = images[0].reshape(size, share, rows, -1).transpose(0, 2, 1, 3)
    valid = valid_mask[0].reshape(size, share, 2, 4).transpose(0, 3, 2, 1)
    valid = valid.reshape(size, 4, 2 * share).astype(jnp.bfloat16)
    valid = jnp.pad(valid, ((0, 0), (0, EXTRA - 4), (0, 256 - 2 * share)))
    sent = jnp.concatenate([x.reshape(size, rows * share, -1), valid], axis=1)
    got = swap(sent, "sp")
    pooled_rows = encode(got, conv_first[0], conv_second[0], share)
    pooled = spread(pooled_rows, "sp").reshape(samples, CH)

    onehot = (scene_index[:, None] == jnp.arange(SCENES, dtype=jnp.int32)[None, :]).astype(
        jnp.float32
    )
    counts = jnp.sum(onehot, axis=0)
    feat = jnp.dot(pooled, project[0], preferred_element_type=jnp.float32)
    sums = jnp.dot(onehot.T, feat, precision=lax.Precision.HIGHEST)
    means = sums / jnp.maximum(counts, 1.0)[:, None]
    panel = (feat - jnp.dot(onehot, means, precision=lax.Precision.HIGHEST)).astype(jnp.bfloat16)
    raw = jnp.dot(panel, whiten[0], preferred_element_type=jnp.float32)
    scale = 1.0 / jnp.sqrt(jnp.mean(raw * raw, axis=-1, keepdims=True) + 1e-05)
    view = (raw * scale).astype(jnp.bfloat16)

    view_rows = lax.dynamic_slice_in_dim(view, first_row, share, 0)
    scale_rows = lax.dynamic_slice_in_dim(scale, first_row, share, 0)
    inner_part = lax.dot_general(
        view_rows, view, (((1,), (1,)), ((), ())), preferred_element_type=jnp.float32
    )
    inner_high = inner_part.astype(jnp.bfloat16)
    inner_low = (inner_part - inner_high.astype(jnp.float32)).astype(jnp.bfloat16)
    few = share // mods * samples // CH
    block = samples // mods
    pieces = jnp.concatenate(
        [
            view.reshape(mods, block, CH),
            inner_high.reshape(mods, few, CH),
            inner_low.reshape(mods, few, CH),
        ],
        axis=1,
    )
    pieces = swap(pieces, "mod").astype(jnp.float32)
    part = jnp.concatenate(
        [
            jnp.sum(pieces[:, :block], axis=0),
            jnp.sum(pieces[:, block : block + few] + pieces[:, block + few :], axis=0),
        ],
        axis=0,
    )
    sums = spread(part, "mod")
    total = sums[:, :block].reshape(samples, CH)
    inner_rows = sums[:, block:].reshape(share, samples)

    eye = jnp.eye(CH, dtype=jnp.float32)
    mean_view = total / mods
    gram = jnp.dot(mean_view.T, mean_view, precision=lax.Precision.HIGHEST) / samples + 0.001 * eye
    lower = jnp.linalg.cholesky(gram)
    total_rows = lax.dynamic_slice_in_dim(total, first_row, share, 0)
    mean_rows = total_rows / mods
    target_rows = jax.scipy.linalg.solve_triangular(lower, mean_rows.T, lower=True).T
    view_f = view_rows.astype(jnp.float32)
    coupling = (
        jnp.dot(inner_rows, view.astype(jnp.float32), precision=lax.Precision.HIGHEST) / samples
        - total_rows
    )
    grad_full = view_f - target_rows + coupling
    inner = jnp.mean(grad_full * view_f, axis=-1, keepdims=True)
    grad_raw = ((grad_full - view_f * inner) * scale_rows).astype(jnp.bfloat16)
    grad_raw_all = spread(grad_raw, "sp").reshape(samples, CH)
    wide = whiten.shape[1] // size
    panel_own = lax.dynamic_slice_in_dim(panel, place * wide, wide, 1)
    grad_w = lax.dot_general(
        panel_own, grad_raw_all, (((0,), (0,)), ((), ())), preferred_element_type=jnp.float32
    )
    return (target_rows, grad_full.astype(jnp.bfloat16)[None], grad_w[None])


def solution(mesh):
    placed = (
        P("mod", None, "sp", None),
        P("mod", None, None),
        P("mod", None, None),
        P("mod", None, None),
        P("mod", None, None),
        P("mod", None, "sp", None),
        P(),
    )
    return jax.shard_map(
        on_device,
        mesh=mesh,
        in_specs=placed,
        out_specs=(P("sp", None), P("mod", "sp", None), P("mod", "sp", None)),
        check_vma=False,
    )
```

```python
import jax
import jax.numpy as jnp
from jax import lax
from jax.experimental import pallas as pl
from jax.experimental.pallas import tpu as pltpu
from jax.sharding import PartitionSpec as P

BANDS = 16
CH = 256
SCENES = 64
EXTRA = 8
TILE = 8
BLOCK = 64


def conv_kernel(got_ref, w1_ref, w2_ref, out_ref, padded_ref, band_ref, first_ref):
    sources = got_ref.shape[0]
    share = out_ref.shape[1]
    rows = (got_ref.shape[1] - EXTRA) // share
    window = 4 * BANDS
    groups = ((0, (0, 1, 2)), (64, (3, 4)), (128, (5, 6, 7)))
    band_ref[...] = jnp.zeros_like(band_ref)
    for start, columns in groups:
        for column in columns:
            low = 2 * BANDS * column - BANDS
            begin, end = (max(low, 0), min(low + window, 256))
            for tap in range(4):
                band_ref[
                    tap * 128 + begin - start : tap * 128 + end - start,
                    column * CH : (column + 1) * CH,
                ] = w1_ref[tap * window + begin - low : tap * window + end - low, :]

    total_rows = sources * rows
    blank = jnp.zeros((share, 256), jnp.bfloat16)
    padded_ref[0, 0] = blank
    padded_ref[total_rows // 2, 1] = blank
    for source in range(sources):
        for row in range(rows):
            place = source * rows + row + 1
            padded_ref[place // 2, place % 2] = got_ref[source, row * share : (row + 1) * share, :]
    blank = jnp.zeros((share, 8 * CH), jnp.bfloat16)
    first_ref[0, 0] = blank
    first_ref[total_rows // 4, 1] = blank

    def first_rows(group, carry):
        for start, columns in groups:
            left = jnp.concatenate(
                [
                    padded_ref[
                        pl.ds(group * 8 + tap // 2, 8), tap % 2, :, start : start + 128
                    ].reshape(8 * share, 128)
                    for tap in range(4)
                ],
                axis=1,
            )
            lanes = slice(columns[0] * CH, (columns[-1] + 1) * CH)
            total = jnp.dot(left, band_ref[:, lanes], preferred_element_type=jnp.float32)
            total = jnp.maximum(total, 0.0).astype(jnp.bfloat16)
            for row in range(8):
                first_ref[group * 4 + (row + 1) // 2, (row + 1) % 2, :, lanes] = total[
                    row * share : (row + 1) * share
                ]
        return carry

    lax.fori_loop(0, total_rows // 16, first_rows, 0)

    span = 8 * share
    spot = lax.broadcasted_iota(jnp.int32, (share, span), 1) % share
    mine = spot == lax.broadcasted_iota(jnp.int32, (share, span), 0)
    pooled = jnp.zeros((share, CH), jnp.float32)
    for group in range(total_rows // 32):
        for column in range(4):
            low, high = (max(2 * column - 1, 0), min(2 * column + 3, 8))
            skip = low - (2 * column - 1)
            total = None
            for tap in range(4):
                left = first_ref[
                    group * 8 + tap // 2 : group * 8 + tap // 2 + 8, tap % 2, :, low * CH : high * CH
                ]
                part = jnp.dot(
                    left.reshape(span, (high - low) * CH),
                    w2_ref[(tap * 4 + skip) * CH : (tap * 4 + skip + high - low) * CH, :],
                    preferred_element_type=jnp.float32,
                )
                total = part if total is None else total + part
            pixel = jnp.maximum(total, 0.0).astype(jnp.bfloat16)
            row = rows * share + column
            valid = jnp.concatenate(
                [
                    got_ref[group * 4 + source, row : row + 1, : 2 * share].astype(jnp.float32)
                    for source in range(4)
                ],
                axis=1,
            )
            chosen = jnp.where(mine, valid, 0.0).astype(jnp.bfloat16)
            pooled = pooled + jnp.dot(chosen, pixel, preferred_element_type=jnp.float32)
    cells = total_rows // 4 * 4
    pooled = (pooled / cells).astype(jnp.bfloat16)
    for source in range(sources):
        out_ref[source] = pooled


def encode(got, w1, w2, share):
    rows = got.shape[0] * (got.shape[1] - EXTRA) // share
    vmem = pl.BlockSpec(memory_space=pltpu.VMEM)
    return pl.pallas_call(
        conv_kernel,
        out_shape=jax.ShapeDtypeStruct((got.shape[0], share, CH), jnp.bfloat16),
        in_specs=[vmem] * 3,
        out_specs=vmem,
        scratch_shapes=[
            pltpu.VMEM((rows // 2 + 1, 2, share, 256), jnp.bfloat16),
            pltpu.VMEM((512, 8 * CH), jnp.bfloat16),
            pltpu.VMEM((rows // 4 + 1, 2, share, 8 * CH), jnp.bfloat16),
        ],
        compiler_params=pltpu.CompilerParams(vmem_limit_bytes=56 * 1024 * 1024),
        name="encode",
    )(got, w1, w2)


def view_kernel(
    place_ref, pooled_ref, project_ref, whiten_ref, scene_ref, panel_ref, view_ref, scale_ref, out_ref
):
    samples = pooled_ref.shape[0]
    share = scale_ref.shape[0]
    mods = out_ref.shape[0]
    block = samples // mods
    exact = lax.Precision.HIGHEST
    feat = jnp.dot(pooled_ref[...], project_ref[...], preferred_element_type=jnp.float32)
    scene = lax.broadcasted_iota(jnp.int32, (SCENES, samples), 0)
    onehot = jnp.where(scene == scene_ref[...], 1.0, 0.0)
    counts = jnp.sum(onehot, axis=1, keepdims=True)
    sums = jnp.dot(onehot, feat, precision=exact, preferred_element_type=jnp.float32)
    means = sums / jnp.maximum(counts, 1.0)
    own = lax.dot_general(
        onehot,
        means,
        (((0,), (0,)), ((), ())),
        precision=exact,
        preferred_element_type=jnp.float32,
    )
    panel = (feat - own).astype(jnp.bfloat16)
    panel_ref[...] = panel
    raw = jnp.dot(panel, whiten_ref[...], preferred_element_type=jnp.float32)
    scale = lax.rsqrt(jnp.mean(raw * raw, axis=-1, keepdims=True) + 1e-05)
    view = (raw * scale).astype(jnp.bfloat16)
    view_ref[...] = view
    out_ref[:, :block, :] = view.reshape(mods, block, CH)
    rows = pl.ds(pl.multiple_of(place_ref[0] * share, share), share)
    mine = view_ref[rows, :]
    raw_rows = jnp.dot(panel_ref[rows, :], whiten_ref[...], preferred_element_type=jnp.float32)
    scale_rows = lax.rsqrt(jnp.mean(raw_rows * raw_rows, axis=-1, keepdims=True) + 1e-05)
    scale_ref[...] = jnp.broadcast_to(scale_rows, scale_ref.shape)
    inner = lax.dot_general(
        mine, view, (((1,), (1,)), ((), ())), preferred_element_type=jnp.float32
    )
    halves = jnp.concatenate([inner[:, :CH], inner[:, CH:]], axis=0).reshape(mods, -1, CH)
    high = halves.astype(jnp.bfloat16).astype(jnp.float32)
    out_ref[:, block:, :] = jnp.concatenate([high, halves - high], axis=1).astype(jnp.bfloat16)


def make_view(place, pooled, project, whiten, scene, share, mods):
    samples = pooled.shape[0]
    half = 2 * share // mods
    vmem = pl.BlockSpec(memory_space=pltpu.VMEM)
    return pl.pallas_call(
        view_kernel,
        out_shape=(
            jax.ShapeDtypeStruct((samples, whiten.shape[0]), jnp.bfloat16),
            jax.ShapeDtypeStruct((samples, CH), jnp.bfloat16),
            jax.ShapeDtypeStruct((share, CH), jnp.float32),
            jax.ShapeDtypeStruct((mods, samples // mods + 2 * half, CH), jnp.bfloat16),
        ),
        in_specs=[pl.BlockSpec(memory_space=pltpu.SMEM)] + [vmem] * 4,
        out_specs=(vmem,) * 4,
        name="view",
    )(place, pooled, project, whiten, scene)


def pivot_inverse(columns):
    low = {}
    for j in range(TILE):
        for i in range(j, TILE):
            low[i, j] = jnp.broadcast_to(columns[j][i : i + 1, :], (TILE, 128))
    inverse = {}
    for j in range(TILE):
        root = lax.rsqrt(low[j, j])
        inverse[j, j] = root
        for i in range(j + 1, TILE):
            low[i, j] = low[i, j] * root
        for m in range(j + 1, TILE):
            for i in range(m, TILE):
                low[i, m] = low[i, m] - low[i, j] * low[m, j]
        for m in range(j):
            total = low[j, m] * inverse[m, m]
            for p in range(m + 1, j):
                total = total + low[j, p] * inverse[p, m]
            inverse[j, m] = -root * total
    return inverse


def factor_block(work_ref, top):
    tiles = range(top // 128, work_ref.shape[1] // 128)
    groups = BLOCK // TILE
    sub = lax.broadcasted_iota(jnp.int32, (TILE, 128), 0)
    rows = {}
    for g in range(groups):
        for t in tiles:
            rows[g, t] = work_ref[
                top + g * TILE : top + (g + 1) * TILE, t * 128 : (t + 1) * 128
            ]

    def lanes(g, tile, lane):
        return [
            jnp.broadcast_to(rows[g, tile][:, lane + j : lane + j + 1], (TILE, 128))
            for j in range(TILE)
        ]

    for g in range(groups):
        at = top + g * TILE
        tile, lane = (at // 128, at % 128)
        inverse = pivot_inverse(lanes(g, tile, lane))
        done = {}
        for j in range(TILE):
            column = inverse[TILE - 1, j]
            for i in range(TILE - 2, j - 1, -1):
                column = jnp.where(sub == i, inverse[i, j], column)
            if j:
                column = jnp.where(sub < j, 0.0, column)
            for t in tiles:
                if (t + 1) * 128 <= at:
                    continue
                part = column * jnp.broadcast_to(rows[g, t][j : j + 1, :], (TILE, 128))
                done[t] = part if j == 0 else done[t] + part
        for t in done:
            work_ref[at : at + TILE, t * 128 : (t + 1) * 128] = done[t]
        spreads = {
            (j, t): jnp.broadcast_to(done[t][j : j + 1, :], (TILE, 128))
            for t in done
            for j in range(TILE)
        }
        for h in range(g + 1, groups):
            columns = lanes(h, tile, lane)
            for j in range(TILE):
                weight = columns[0] * inverse[j, 0]
                for m in range(1, j + 1):
                    weight = weight + columns[m] * inverse[j, m]
                for t in done:
                    rows[h, t] = rows[h, t] - weight * spreads[j, t]


def solve(work_ref):
    size = work_ref.shape[0]
    for top in range(0, size, BLOCK):
        factor_block(work_ref, top)
        low = top + BLOCK
        if low < size:
            start = low // 128 * 128
            change = lax.dot_general(
                work_ref[top:low, start:size],
                work_ref[top:low, start:],
                (((0,), (0,)), ((), ())),
                precision=lax.Precision.HIGHEST,
                preferred_element_type=jnp.float32,
            )
            work_ref[low:, start:] = work_ref[low:, start:] - change[low - start :]


def tail_kernel(
    place_ref, sums_ref, view_ref, scale_ref, target_ref, view_grad_ref, raw_grad_ref, work_ref
):
    samples, width = view_ref.shape
    share = scale_ref.shape[0]
    mods = sums_ref.shape[0]
    block = samples // mods
    owners = share // block
    total = sums_ref[:, :block, :].reshape(samples, width)
    mine = sums_ref[pl.ds(place_ref[0] * owners, owners), :block, :].reshape(share, width)
    gram = lax.dot_general(
        total,
        total,
        (((0,), (0,)), ((), ())),
        precision=lax.Precision.HIGHEST,
        preferred_element_type=jnp.float32,
    )
    shape = (width, width)
    eye = lax.broadcasted_iota(jnp.int32, shape, 0) == lax.broadcasted_iota(jnp.int32, shape, 1)
    work_ref[:, :width] = gram / (mods * mods * samples) + jnp.where(eye, 0.001, 0.0)
    blank = jnp.zeros((128 - share, width), jnp.float32)
    work_ref[:, width:] = jnp.concatenate([mine / mods, blank], axis=0).T
    solve(work_ref)
    target = work_ref[:, width:].T[:share]
    target_ref[...] = target

    def times(left, right):
        high = left.astype(jnp.bfloat16)
        low = (left - high.astype(jnp.float32)).astype(jnp.bfloat16)
        return jnp.dot(high, right, preferred_element_type=jnp.float32) + jnp.dot(
            low, right, preferred_element_type=jnp.float32
        )

    inner = sums_ref[:, block:, :].reshape(2 * share, width)
    coupling = times(inner[:share], view_ref[:width, :]) + times(inner[share:], view_ref[width:, :])
    coupling = coupling / samples - mine
    rows = pl.ds(pl.multiple_of(place_ref[0] * share, share), share)
    view = view_ref[rows, :].astype(jnp.float32)
    grad = view - target + coupling
    view_grad_ref[...] = grad.astype(jnp.bfloat16)
    mean = jnp.mean(grad * view, axis=-1, keepdims=True)
    raw_grad = ((grad - view * mean) * scale_ref[...]).astype(jnp.bfloat16)
    for source in range(raw_grad_ref.shape[0]):
        raw_grad_ref[source] = raw_grad


def finish(place, sums, view, scale, size):
    width = view.shape[1]
    share = scale.shape[0]
    vmem = pl.BlockSpec(memory_space=pltpu.VMEM)
    return pl.pallas_call(
        tail_kernel,
        out_shape=(
            jax.ShapeDtypeStruct((share, width), jnp.float32),
            jax.ShapeDtypeStruct((share, width), jnp.bfloat16),
            jax.ShapeDtypeStruct((size, share, width), jnp.bfloat16),
        ),
        in_specs=[pl.BlockSpec(memory_space=pltpu.SMEM)] + [vmem] * 3,
        out_specs=(vmem,) * 3,
        scratch_shapes=[pltpu.VMEM((width, width + 128), jnp.float32)],
        name="finish",
    )(place, sums, view, scale)


def swap(x, axis):
    return lax.all_to_all(x, axis, 0, 0, tiled=True)


def spread(x, axis):
    return swap(jnp.broadcast_to(x[None], (lax.axis_size(axis),) + x.shape), axis)


def on_device(images, conv_first, conv_second, project, whiten, valid_mask, scene_index):
    samples = images.shape[1]
    size = lax.axis_size("sp")
    mods = lax.axis_size("mod")
    place = lax.axis_index("sp")
    share = samples // size
    rows = images.shape[2]
    x = images[0].reshape(size, share, rows, -1).transpose(0, 2, 1, 3)
    valid = valid_mask[0].reshape(size, share, 2, 4).transpose(0, 3, 2, 1)
    valid = valid.reshape(size, 4, 2 * share).astype(jnp.bfloat16)
    valid = jnp.pad(valid, ((0, 0), (0, EXTRA - 4), (0, 256 - 2 * share)))
    sent = jnp.concatenate([x.reshape(size, rows * share, -1), valid], axis=1)
    got = swap(sent, "sp")
    pooled = encode(got, conv_first[0], conv_second[0], share)
    pooled = swap(pooled, "sp").reshape(samples, CH)

    spot = place.reshape(1)
    panel, view, scale_rows, pieces = make_view(
        spot, pooled, project[0], whiten[0], scene_index.reshape(1, samples), share, mods
    )
    pieces = swap(pieces, "mod").astype(jnp.float32)
    block = samples // mods
    few = 2 * share // mods
    part = jnp.concatenate(
        [
            jnp.sum(pieces[:, :block], axis=0),
            jnp.sum(pieces[:, block : block + few] + pieces[:, block + few :], axis=0),
        ],
        axis=0,
    )
    sums = spread(part, "mod")
    target_rows, view_grad, raw_grad = finish(spot, sums, view, scale_rows, size)
    raw_grad = swap(raw_grad, "sp").reshape(samples, CH)
    wide = whiten.shape[1] // size
    panel_own = lax.dynamic_slice_in_dim(panel, place * wide, wide, 1)
    grad_w = lax.dot_general(
        panel_own, raw_grad, (((0,), (0,)), ((), ())), preferred_element_type=jnp.float32
    )
    return (target_rows, view_grad[None], grad_w[None])


def solution(mesh):
    placed = (
        P("mod", None, "sp", None),
        P("mod", None, None),
        P("mod", None, None),
        P("mod", None, None),
        P("mod", None, None),
        P("mod", None, "sp", None),
        P(),
    )
    return jax.shard_map(
        on_device,
        mesh=mesh,
        in_specs=placed,
        out_specs=(P("sp", None), P("mod", "sp", None), P("mod", "sp", None)),
        check_vma=False,
    )
```

```python
import jax
import jax.numpy as jnp
from jax import lax
from jax.experimental import pallas as pl
from jax.experimental.pallas import tpu as pltpu
from jax.sharding import PartitionSpec as P

BANDS = 16
CH = 256
SCENES = 64
MODS = 16
EXTRA = 8
TILE = 8
BLOCK = 64


def conv_kernel(got_ref, w1_ref, w2_ref, out_ref, padded_ref, band_ref, first_ref):
    sources = got_ref.shape[0]
    share = out_ref.shape[1]
    rows = (got_ref.shape[1] - EXTRA) // share
    window = 4 * BANDS
    groups = ((0, (0, 1, 2)), (64, (3, 4)), (128, (5, 6, 7)))
    band_ref[...] = jnp.zeros_like(band_ref)
    for start, columns in groups:
        for column in columns:
            low = 2 * BANDS * column - BANDS
            begin, end = (max(low, 0), min(low + window, 256))
            for tap in range(4):
                band_ref[
                    tap * 128 + begin - start : tap * 128 + end - start,
                    column * CH : (column + 1) * CH,
                ] = w1_ref[tap * window + begin - low : tap * window + end - low, :]

    total_rows = sources * rows
    blank = jnp.zeros((share, 256), jnp.bfloat16)
    padded_ref[0, 0] = blank
    padded_ref[total_rows // 2, 1] = blank
    for source in range(sources):
        for row in range(rows):
            place = source * rows + row + 1
            padded_ref[place // 2, place % 2] = got_ref[source, row * share : (row + 1) * share, :]
    blank = jnp.zeros((share, 8 * CH), jnp.bfloat16)
    first_ref[0, 0] = blank
    first_ref[total_rows // 4, 1] = blank

    def first_rows(group, carry):
        for start, columns in groups:
            left = jnp.concatenate(
                [
                    padded_ref[
                        pl.ds(group * 8 + tap // 2, 8), tap % 2, :, start : start + 128
                    ].reshape(8 * share, 128)
                    for tap in range(4)
                ],
                axis=1,
            )
            lanes = slice(columns[0] * CH, (columns[-1] + 1) * CH)
            total = jnp.dot(left, band_ref[:, lanes], preferred_element_type=jnp.float32)
            total = jnp.maximum(total, 0.0).astype(jnp.bfloat16)
            for row in range(8):
                first_ref[group * 4 + (row + 1) // 2, (row + 1) % 2, :, lanes] = total[
                    row * share : (row + 1) * share
                ]
        return carry

    lax.fori_loop(0, total_rows // 16, first_rows, 0)

    span = 8 * share
    spot = lax.broadcasted_iota(jnp.int32, (share, span), 1) % share
    mine = spot == lax.broadcasted_iota(jnp.int32, (share, span), 0)
    pooled = jnp.zeros((share, CH), jnp.float32)
    for group in range(total_rows // 32):
        for column in range(4):
            low, high = (max(2 * column - 1, 0), min(2 * column + 3, 8))
            skip = low - (2 * column - 1)
            total = None
            for tap in range(4):
                left = first_ref[
                    group * 8 + tap // 2 : group * 8 + tap // 2 + 8, tap % 2, :, low * CH : high * CH
                ]
                part = jnp.dot(
                    left.reshape(span, (high - low) * CH),
                    w2_ref[(tap * 4 + skip) * CH : (tap * 4 + skip + high - low) * CH, :],
                    preferred_element_type=jnp.float32,
                )
                total = part if total is None else total + part
            pixel = jnp.maximum(total, 0.0).astype(jnp.bfloat16)
            row = rows * share + column
            valid = jnp.concatenate(
                [
                    got_ref[group * 4 + source, row : row + 1, : 2 * share].astype(jnp.float32)
                    for source in range(4)
                ],
                axis=1,
            )
            chosen = jnp.where(mine, valid, 0.0).astype(jnp.bfloat16)
            pooled = pooled + jnp.dot(chosen, pixel, preferred_element_type=jnp.float32)
    cells = total_rows // 4 * 4
    pooled = (pooled / cells).astype(jnp.bfloat16)
    for source in range(sources):
        out_ref[source] = pooled


def encode(got, w1, w2, share):
    rows = got.shape[0] * (got.shape[1] - EXTRA) // share
    vmem = pl.BlockSpec(memory_space=pltpu.VMEM)
    return pl.pallas_call(
        conv_kernel,
        out_shape=jax.ShapeDtypeStruct((got.shape[0], share, CH), jnp.bfloat16),
        in_specs=[vmem] * 3,
        out_specs=vmem,
        scratch_shapes=[
            pltpu.VMEM((rows // 2 + 1, 2, share, 256), jnp.bfloat16),
            pltpu.VMEM((512, 8 * CH), jnp.bfloat16),
            pltpu.VMEM((rows // 4 + 1, 2, share, 8 * CH), jnp.bfloat16),
        ],
        compiler_params=pltpu.CompilerParams(vmem_limit_bytes=56 * 1024 * 1024),
        name="encode",
    )(got, w1, w2)


def view_kernel(
    place_ref, pooled_ref, project_ref, whiten_ref, scene_ref, columns_ref, view_ref, scale_ref
):
    samples = pooled_ref.shape[0]
    exact = lax.Precision.HIGHEST
    feat = jnp.dot(pooled_ref[...], project_ref[...], preferred_element_type=jnp.float32)
    scene = lax.broadcasted_iota(jnp.int32, (SCENES, samples), 0)
    onehot = jnp.where(scene == scene_ref[...], 1.0, 0.0)
    counts = jnp.sum(onehot, axis=1, keepdims=True)
    sums = jnp.dot(onehot, feat, precision=exact, preferred_element_type=jnp.float32)
    means = sums / jnp.maximum(counts, 1.0)
    own = lax.dot_general(
        onehot,
        means,
        (((0,), (0,)), ((), ())),
        precision=exact,
        preferred_element_type=jnp.float32,
    )
    panel = (feat - own).astype(jnp.bfloat16)
    raw = jnp.dot(panel, whiten_ref[...], preferred_element_type=jnp.float32)
    scale = lax.rsqrt(jnp.mean(raw * raw, axis=-1, keepdims=True) + 1e-05)
    scale_ref[...] = jnp.broadcast_to(scale, scale_ref.shape)
    view_ref[...] = (raw * scale).astype(jnp.bfloat16)
    wide, depth = (columns_ref.shape[0], panel.shape[1])
    feature = lax.broadcasted_iota(jnp.int32, (wide, depth), 1)
    wanted = lax.broadcasted_iota(jnp.int32, (wide, depth), 0) + place_ref[0] * wide
    pick = jnp.where(feature == wanted, 1.0, 0.0).astype(jnp.bfloat16)
    columns = lax.dot_general(
        pick, panel, (((1,), (1,)), ((), ())), preferred_element_type=jnp.float32
    )
    columns_ref[...] = columns.astype(jnp.bfloat16)


def make_view(place, pooled, project, whiten, scene, size):
    samples = pooled.shape[0]
    vmem = pl.BlockSpec(memory_space=pltpu.VMEM)
    return pl.pallas_call(
        view_kernel,
        out_shape=(
            jax.ShapeDtypeStruct((whiten.shape[0] // size, samples), jnp.bfloat16),
            jax.ShapeDtypeStruct((samples, CH), jnp.bfloat16),
            jax.ShapeDtypeStruct((samples, 128), jnp.float32),
        ),
        in_specs=[pl.BlockSpec(memory_space=pltpu.SMEM)] + [vmem] * 4,
        out_specs=(vmem,) * 3,
        name="view",
    )(place, pooled, project, whiten, scene)


def pair_kernel(place_ref, view_ref, other_ref, out_ref):
    chips = out_ref.shape[0]
    half = view_ref.shape[0] // 2
    block = half // chips
    rows = pl.ds(pl.multiple_of(place_ref[1] * half, half), half)
    first, second = (view_ref[rows, :], other_ref[rows, :])
    both = first.astype(jnp.float32) + second.astype(jnp.float32)
    out_ref[:, :block, :] = both.astype(jnp.bfloat16).reshape(chips, block, CH)
    over = (((1,), (1,)), ((), ()))
    inner = lax.dot_general(first, view_ref[...], over, preferred_element_type=jnp.float32)
    inner = inner + lax.dot_general(
        second, other_ref[...], over, preferred_element_type=jnp.float32
    )
    inner = inner.astype(jnp.bfloat16)
    out_ref[:, block : 2 * block, :] = inner[:, :CH].reshape(chips, block, CH)
    out_ref[:, 2 * block :, :] = inner[:, CH:].reshape(chips, block, CH)


def pair_sums(place, view, other, chips):
    vmem = pl.BlockSpec(memory_space=pltpu.VMEM)
    block = view.shape[0] // 2 // chips
    return pl.pallas_call(
        pair_kernel,
        out_shape=jax.ShapeDtypeStruct((chips, 3 * block, CH), jnp.bfloat16),
        in_specs=[pl.BlockSpec(memory_space=pltpu.SMEM), vmem, vmem],
        out_specs=vmem,
        name="pair",
    )(place, view, other)


def sum_kernel(in_ref, out_ref):
    total = in_ref[0].astype(jnp.float32)
    for source in range(1, in_ref.shape[0]):
        total = total + in_ref[source].astype(jnp.float32)
    total = total.astype(jnp.bfloat16)
    for source in range(in_ref.shape[0]):
        out_ref[source] = total


def sum_spread(x):
    vmem = pl.BlockSpec(memory_space=pltpu.VMEM)
    return pl.pallas_call(
        sum_kernel,
        out_shape=jax.ShapeDtypeStruct(x.shape, x.dtype),
        in_specs=[vmem],
        out_specs=vmem,
        name="sums",
    )(x)


def pivot_inverse(columns):
    low = {}
    for j in range(TILE):
        for i in range(j, TILE):
            low[i, j] = jnp.broadcast_to(columns[j][i : i + 1, :], (TILE, 128))
    inverse = {}
    for j in range(TILE):
        root = lax.rsqrt(low[j, j])
        inverse[j, j] = root
        for i in range(j + 1, TILE):
            low[i, j] = low[i, j] * root
        for m in range(j + 1, TILE):
            for i in range(m, TILE):
                low[i, m] = low[i, m] - low[i, j] * low[m, j]
        for m in range(j):
            total = low[j, m] * inverse[m, m]
            for p in range(m + 1, j):
                total = total + low[j, p] * inverse[p, m]
            inverse[j, m] = -root * total
    return inverse


def factor_block(work_ref, top):
    half = work_ref.shape[1] // 256
    tiles = [t for t in range(top // 128, 2 * half) if t < half or (t - half) * 128 <= top]
    groups = BLOCK // TILE
    sub = lax.broadcasted_iota(jnp.int32, (TILE, 128), 0)
    rows = {}
    for g in range(groups):
        for t in tiles:
            rows[g, t] = work_ref[
                top + g * TILE : top + (g + 1) * TILE, t * 128 : (t + 1) * 128
            ]

    def lanes(g, tile, lane):
        return [
            jnp.broadcast_to(rows[g, tile][:, lane + j : lane + j + 1], (TILE, 128))
            for j in range(TILE)
        ]

    for g in range(groups):
        at = top + g * TILE
        tile, lane = (at // 128, at % 128)
        inverse = pivot_inverse(lanes(g, tile, lane))
        done = {}
        for j in range(TILE):
            column = inverse[TILE - 1, j]
            for i in range(TILE - 2, j - 1, -1):
                column = jnp.where(sub == i, inverse[i, j], column)
            if j:
                column = jnp.where(sub < j, 0.0, column)
            for t in tiles:
                part = column * jnp.broadcast_to(rows[g, t][j : j + 1, :], (TILE, 128))
                done[t] = part if j == 0 else done[t] + part
        for t in done:
            work_ref[at : at + TILE, t * 128 : (t + 1) * 128] = done[t]
        spreads = {
            (j, t): jnp.broadcast_to(done[t][j : j + 1, :], (TILE, 128))
            for t in done
            for j in range(TILE)
        }
        for h in range(g + 1, groups):
            columns = lanes(h, tile, lane)
            for j in range(TILE):
                weight = columns[0] * inverse[j, 0]
                for m in range(1, j + 1):
                    weight = weight + columns[m] * inverse[j, m]
                for t in done:
                    rows[h, t] = rows[h, t] - weight * spreads[j, t]


def solve(work_ref):
    size = work_ref.shape[0]
    for top in range(0, size, BLOCK):
        factor_block(work_ref, top)
        low = top + BLOCK
        if low < size:
            start = low // 128 * 128
            change = lax.dot_general(
                work_ref[top:low, start:size],
                work_ref[top:low, start:],
                (((0,), (0,)), ((), ())),
                precision=lax.Precision.HIGHEST,
                preferred_element_type=jnp.float32,
            )
            work_ref[low:, start:] = work_ref[low:, start:] - change[low - start :]


def tail_kernel(
    place_ref,
    sums_ref,
    other_ref,
    view_ref,
    scale_ref,
    columns_ref,
    target_ref,
    view_grad_ref,
    weight_grad_ref,
    work_ref,
    full_ref,
):
    samples, width = view_ref.shape
    share = target_ref.shape[0]
    block = sums_ref.shape[1] // 3
    half = samples // 2
    core = place_ref[1]

    def whole(part):
        lanes = slice(part * block, (part + 1) * block)
        mine = sums_ref[:, lanes, :].reshape(half, width)
        other = other_ref[:, lanes, :].reshape(half, width)
        return jnp.concatenate(
            [jnp.where(core == 0, mine, other), jnp.where(core == 0, other, mine)], axis=0
        )

    total = whole(0)
    mean = total * (1.0 / MODS)
    gram = lax.dot_general(
        mean, mean, (((0,), (0,)), ((), ())), preferred_element_type=jnp.float32
    )
    shape = (width, width)
    eye = lax.broadcasted_iota(jnp.int32, shape, 0) == lax.broadcasted_iota(jnp.int32, shape, 1)
    work_ref[:, :width] = gram / samples + jnp.where(eye, 0.001, 0.0)
    work_ref[:, width:] = jnp.where(eye, 1.0, 0.0)
    solve(work_ref)
    target = lax.dot_general(
        mean.astype(jnp.float32),
        work_ref[:, width:],
        (((1,), (1,)), ((), ())),
        precision=lax.Precision.HIGHEST,
        preferred_element_type=jnp.float32,
    )
    coupling = jnp.dot(whole(1), view_ref[:width, :], preferred_element_type=jnp.float32)
    coupling = coupling + jnp.dot(whole(2), view_ref[width:, :], preferred_element_type=jnp.float32)
    coupling = coupling / samples - total.astype(jnp.float32)
    view = view_ref[...].astype(jnp.float32)
    grad = view - target + coupling
    share_rows = pl.ds(pl.multiple_of(place_ref[0] * share, share), share)
    full_ref[...] = target
    target_ref[...] = full_ref[share_rows, :]
    full_ref[...] = grad
    view_grad_ref[...] = full_ref[share_rows, :].astype(jnp.bfloat16)
    inner = jnp.mean(grad * view, axis=-1, keepdims=True)
    scale = jnp.concatenate([scale_ref[...]] * (width // 128), axis=1)
    raw_grad = ((grad - view * inner) * scale).astype(jnp.bfloat16)
    weight_grad_ref[...] = jnp.dot(
        columns_ref[...], raw_grad, preferred_element_type=jnp.float32
    )


def finish(place, sums, other, view, scale, columns, share):
    samples, width = view.shape
    vmem = pl.BlockSpec(memory_space=pltpu.VMEM)
    return pl.pallas_call(
        tail_kernel,
        out_shape=(
            jax.ShapeDtypeStruct((share, width), jnp.float32),
            jax.ShapeDtypeStruct((share, width), jnp.bfloat16),
            jax.ShapeDtypeStruct((columns.shape[0], width), jnp.float32),
        ),
        in_specs=[pl.BlockSpec(memory_space=pltpu.SMEM)] + [vmem] * 5,
        out_specs=(vmem,) * 3,
        scratch_shapes=[
            pltpu.VMEM((width, 2 * width), jnp.float32),
            pltpu.VMEM((samples, width), jnp.float32),
        ],
        name="finish",
    )(place, sums, other, view, scale, columns)


def swap(x, axis, groups=None):
    return lax.all_to_all(x, axis, 0, 0, tiled=True, axis_index_groups=groups)


def on_device(images, conv_first, conv_second, project, whiten, valid_mask, scene_index):
    samples = images.shape[1]
    size = lax.axis_size("sp")
    mods = lax.axis_size("mod")
    place = lax.axis_index("sp")
    share = samples // size
    rows = images.shape[2]
    x = images[0].reshape(size, share, rows, -1).transpose(0, 2, 1, 3)
    valid = valid_mask[0].reshape(size, share, 2, 4).transpose(0, 3, 2, 1)
    valid = valid.reshape(size, 4, 2 * share).astype(jnp.bfloat16)
    valid = jnp.pad(valid, ((0, 0), (0, EXTRA - 4), (0, 256 - 2 * share)))
    sent = jnp.concatenate([x.reshape(size, rows * share, -1), valid], axis=1)
    got = swap(sent, "sp")
    pooled = encode(got, conv_first[0], conv_second[0], share)
    pooled = swap(pooled, "sp").reshape(samples, CH)

    spot = jnp.stack([place, lax.axis_index("mod") % 2])
    columns, view, scale = make_view(
        spot, pooled, project[0], whiten[0], scene_index.reshape(1, samples), size
    )
    partner = [(i, i ^ 1) for i in range(mods)]
    chips = [[2 * i + core for i in range(mods // 2)] for core in range(2)]
    pieces = pair_sums(spot, view, lax.ppermute(view, "mod", partner), mods // 2)
    pieces = sum_spread(swap(pieces, "mod", chips))
    sums = swap(pieces, "mod", chips)
    other = lax.ppermute(sums, "mod", partner)
    target_rows, view_grad, grad_w = finish(spot, sums, other, view, scale, columns, share)
    return (target_rows, view_grad[None], grad_w[None])


def solution(mesh):
    placed = (
        P("mod", None, "sp", None),
        P("mod", None, None),
        P("mod", None, None),
        P("mod", None, None),
        P("mod", None, None),
        P("mod", None, "sp", None),
        P(),
    )
    return jax.shard_map(
        on_device,
        mesh=mesh,
        in_specs=placed,
        out_specs=(P("sp", None), P("mod", "sp", None), P("mod", "sp", None)),
        check_vma=False,
    )
```

```python
import jax
import jax.numpy as jnp
from jax import lax
from jax.experimental import pallas as pl
from jax.experimental.pallas import tpu as pltpu
from jax.sharding import PartitionSpec as P

BANDS = 16
CH = 256
SCENES = 64
MODS = 16
EXTRA = 8
TILE = 8
BLOCK = 64


def conv_kernel(got_ref, w1_ref, w2_ref, out_ref, padded_ref, band_ref, first_ref):
    sources = got_ref.shape[0]
    share = out_ref.shape[1]
    rows = (got_ref.shape[1] - EXTRA) // share
    window = 4 * BANDS
    groups = ((0, (0, 1, 2)), (64, (3, 4)), (128, (5, 6, 7)))
    band_ref[...] = jnp.zeros_like(band_ref)
    for start, columns in groups:
        for column in columns:
            low = 2 * BANDS * column - BANDS
            begin, end = (max(low, 0), min(low + window, 256))
            for tap in range(4):
                band_ref[
                    tap * 128 + begin - start : tap * 128 + end - start,
                    column * CH : (column + 1) * CH,
                ] = w1_ref[tap * window + begin - low : tap * window + end - low, :]

    total_rows = sources * rows
    blank = jnp.zeros((share, 256), jnp.bfloat16)
    padded_ref[0, 0] = blank
    padded_ref[total_rows // 2, 1] = blank
    for source in range(sources):
        for row in range(rows):
            place = source * rows + row + 1
            padded_ref[place // 2, place % 2] = got_ref[source, row * share : (row + 1) * share, :]
    blank = jnp.zeros((share, 8 * CH), jnp.bfloat16)
    first_ref[0, 0] = blank
    first_ref[total_rows // 4, 1] = blank

    def first_rows(group, carry):
        for start, columns in groups:
            left = jnp.concatenate(
                [
                    padded_ref[
                        pl.ds(group * 8 + tap // 2, 8), tap % 2, :, start : start + 128
                    ].reshape(8 * share, 128)
                    for tap in range(4)
                ],
                axis=1,
            )
            lanes = slice(columns[0] * CH, (columns[-1] + 1) * CH)
            total = jnp.dot(left, band_ref[:, lanes], preferred_element_type=jnp.float32)
            total = jnp.maximum(total, 0.0).astype(jnp.bfloat16)
            for row in range(8):
                first_ref[group * 4 + (row + 1) // 2, (row + 1) % 2, :, lanes] = total[
                    row * share : (row + 1) * share
                ]
        return carry

    lax.fori_loop(0, total_rows // 16, first_rows, 0)

    span = 8 * share
    spot = lax.broadcasted_iota(jnp.int32, (share, span), 1) % share
    mine = spot == lax.broadcasted_iota(jnp.int32, (share, span), 0)
    pooled = jnp.zeros((share, CH), jnp.float32)
    for group in range(total_rows // 32):
        for column in range(4):
            low, high = (max(2 * column - 1, 0), min(2 * column + 3, 8))
            skip = low - (2 * column - 1)
            total = None
            for tap in range(4):
                left = first_ref[
                    group * 8 + tap // 2 : group * 8 + tap // 2 + 8, tap % 2, :, low * CH : high * CH
                ]
                part = jnp.dot(
                    left.reshape(span, (high - low) * CH),
                    w2_ref[(tap * 4 + skip) * CH : (tap * 4 + skip + high - low) * CH, :],
                    preferred_element_type=jnp.float32,
                )
                total = part if total is None else total + part
            pixel = jnp.maximum(total, 0.0).astype(jnp.bfloat16)
            row = rows * share + column
            valid = jnp.concatenate(
                [
                    got_ref[group * 4 + source, row : row + 1, : 2 * share].astype(jnp.float32)
                    for source in range(4)
                ],
                axis=1,
            )
            chosen = jnp.where(mine, valid, 0.0).astype(jnp.bfloat16)
            pooled = pooled + jnp.dot(chosen, pixel, preferred_element_type=jnp.float32)
    cells = total_rows // 4 * 4
    pooled = (pooled / cells).astype(jnp.bfloat16)
    for source in range(sources):
        out_ref[source] = pooled


def encode(got, w1, w2, share):
    rows = got.shape[0] * (got.shape[1] - EXTRA) // share
    vmem = pl.BlockSpec(memory_space=pltpu.VMEM)
    return pl.pallas_call(
        conv_kernel,
        out_shape=jax.ShapeDtypeStruct((got.shape[0], share, CH), jnp.bfloat16),
        in_specs=[vmem] * 3,
        out_specs=vmem,
        scratch_shapes=[
            pltpu.VMEM((rows // 2 + 1, 2, share, 256), jnp.bfloat16),
            pltpu.VMEM((512, 8 * CH), jnp.bfloat16),
            pltpu.VMEM((rows // 4 + 1, 2, share, 8 * CH), jnp.bfloat16),
        ],
        compiler_params=pltpu.CompilerParams(vmem_limit_bytes=24 * 1024 * 1024),
        name="encode",
    )(got, w1, w2)


def view_kernel(
    place_ref, pooled_ref, project_ref, whiten_ref, scene_ref, columns_ref, view_ref, scale_ref
):
    samples = pooled_ref.shape[0]
    exact = lax.Precision.HIGHEST
    feat = jnp.dot(pooled_ref[...], project_ref[...], preferred_element_type=jnp.float32)
    scene = lax.broadcasted_iota(jnp.int32, (SCENES, samples), 0)
    onehot = jnp.where(scene == scene_ref[...], 1.0, 0.0)
    counts = jnp.sum(onehot, axis=1, keepdims=True)
    sums = jnp.dot(onehot, feat, precision=exact, preferred_element_type=jnp.float32)
    means = sums / jnp.maximum(counts, 1.0)
    own = lax.dot_general(
        onehot,
        means,
        (((0,), (0,)), ((), ())),
        precision=exact,
        preferred_element_type=jnp.float32,
    )
    panel = (feat - own).astype(jnp.bfloat16)
    raw = jnp.dot(panel, whiten_ref[...], preferred_element_type=jnp.float32)
    scale = lax.rsqrt(jnp.mean(raw * raw, axis=-1, keepdims=True) + 1e-05)
    scale_ref[...] = jnp.broadcast_to(scale, scale_ref.shape)
    view_ref[...] = (raw * scale).astype(jnp.bfloat16)
    wide, depth = (columns_ref.shape[0], panel.shape[1])
    feature = lax.broadcasted_iota(jnp.int32, (wide, depth), 1)
    wanted = lax.broadcasted_iota(jnp.int32, (wide, depth), 0) + place_ref[0] * wide
    pick = jnp.where(feature == wanted, 1.0, 0.0).astype(jnp.bfloat16)
    columns = lax.dot_general(
        pick, panel, (((1,), (1,)), ((), ())), preferred_element_type=jnp.float32
    )
    columns_ref[...] = columns.astype(jnp.bfloat16)


def make_view(place, pooled, project, whiten, scene, size):
    samples = pooled.shape[0]
    vmem = pl.BlockSpec(memory_space=pltpu.VMEM)
    return pl.pallas_call(
        view_kernel,
        out_shape=(
            jax.ShapeDtypeStruct((whiten.shape[0] // size, samples), jnp.bfloat16),
            jax.ShapeDtypeStruct((samples, CH), jnp.bfloat16),
            jax.ShapeDtypeStruct((samples, 128), jnp.float32),
        ),
        in_specs=[pl.BlockSpec(memory_space=pltpu.SMEM)] + [vmem] * 4,
        out_specs=(vmem,) * 3,
        compiler_params=pltpu.CompilerParams(vmem_limit_bytes=12 * 1024 * 1024),
        name="view",
    )(place, pooled, project, whiten, scene)


def pair_kernel(place_ref, view_ref, other_ref, out_ref):
    chips = out_ref.shape[0]
    half = view_ref.shape[0] // 2
    block = half // chips
    rows = pl.ds(pl.multiple_of(place_ref[1] * half, half), half)
    first, second = (view_ref[rows, :], other_ref[rows, :])
    both = first.astype(jnp.float32) + second.astype(jnp.float32)
    out_ref[:, :block, :] = both.astype(jnp.bfloat16).reshape(chips, block, CH)
    over = (((1,), (1,)), ((), ()))
    inner = lax.dot_general(first, view_ref[...], over, preferred_element_type=jnp.float32)
    inner = inner + lax.dot_general(
        second, other_ref[...], over, preferred_element_type=jnp.float32
    )
    inner = inner.astype(jnp.bfloat16)
    out_ref[:, block : 2 * block, :] = inner[:, :CH].reshape(chips, block, CH)
    out_ref[:, 2 * block :, :] = inner[:, CH:].reshape(chips, block, CH)


def pair_sums(place, view, other, chips):
    vmem = pl.BlockSpec(memory_space=pltpu.VMEM)
    block = view.shape[0] // 2 // chips
    return pl.pallas_call(
        pair_kernel,
        out_shape=jax.ShapeDtypeStruct((chips, 3 * block, CH), jnp.bfloat16),
        in_specs=[pl.BlockSpec(memory_space=pltpu.SMEM), vmem, vmem],
        out_specs=vmem,
        compiler_params=pltpu.CompilerParams(vmem_limit_bytes=8 * 1024 * 1024),
        name="pair",
    )(place, view, other)


def sum_kernel(in_ref, out_ref):
    total = in_ref[0].astype(jnp.float32)
    for source in range(1, in_ref.shape[0]):
        total = total + in_ref[source].astype(jnp.float32)
    total = total.astype(jnp.bfloat16)
    for source in range(in_ref.shape[0]):
        out_ref[source] = total


def sum_spread(x):
    vmem = pl.BlockSpec(memory_space=pltpu.VMEM)
    return pl.pallas_call(
        sum_kernel,
        out_shape=jax.ShapeDtypeStruct(x.shape, x.dtype),
        in_specs=[vmem],
        out_specs=vmem,
        compiler_params=pltpu.CompilerParams(vmem_limit_bytes=6 * 1024 * 1024),
        name="sums",
    )(x)


def pivot_inverse(columns):
    low = {}
    for j in range(TILE):
        for i in range(j, TILE):
            low[i, j] = jnp.broadcast_to(columns[j][i : i + 1, :], (TILE, 128))
    inverse = {}
    for j in range(TILE):
        root = lax.rsqrt(low[j, j])
        inverse[j, j] = root
        for i in range(j + 1, TILE):
            low[i, j] = low[i, j] * root
        for m in range(j + 1, TILE):
            for i in range(m, TILE):
                low[i, m] = low[i, m] - low[i, j] * low[m, j]
        for m in range(j):
            total = low[j, m] * inverse[m, m]
            for p in range(m + 1, j):
                total = total + low[j, p] * inverse[p, m]
            inverse[j, m] = -root * total
    return inverse


def factor_block(work_ref, top):
    half = work_ref.shape[1] // 256
    tiles = [t for t in range(top // 128, 2 * half) if t < half or (t - half) * 128 <= top]
    groups = BLOCK // TILE
    sub = lax.broadcasted_iota(jnp.int32, (TILE, 128), 0)
    rows = {}
    for g in range(groups):
        for t in tiles:
            rows[g, t] = work_ref[
                top + g * TILE : top + (g + 1) * TILE, t * 128 : (t + 1) * 128
            ]

    def lanes(g, tile, lane):
        return [
            jnp.broadcast_to(rows[g, tile][:, lane + j : lane + j + 1], (TILE, 128))
            for j in range(TILE)
        ]

    for g in range(groups):
        at = top + g * TILE
        tile, lane = (at // 128, at % 128)
        inverse = pivot_inverse(lanes(g, tile, lane))
        done = {}
        for j in range(TILE):
            column = inverse[TILE - 1, j]
            for i in range(TILE - 2, j - 1, -1):
                column = jnp.where(sub == i, inverse[i, j], column)
            if j:
                column = jnp.where(sub < j, 0.0, column)
            for t in tiles:
                part = column * jnp.broadcast_to(rows[g, t][j : j + 1, :], (TILE, 128))
                done[t] = part if j == 0 else done[t] + part
        for t in done:
            work_ref[at : at + TILE, t * 128 : (t + 1) * 128] = done[t]
        spreads = {
            (j, t): jnp.broadcast_to(done[t][j : j + 1, :], (TILE, 128))
            for t in done
            for j in range(TILE)
        }
        for h in range(g + 1, groups):
            columns = lanes(h, tile, lane)
            for j in range(TILE):
                weight = columns[0] * inverse[j, 0]
                for m in range(1, j + 1):
                    weight = weight + columns[m] * inverse[j, m]
                for t in done:
                    rows[h, t] = rows[h, t] - weight * spreads[j, t]


def solve(work_ref):
    size = work_ref.shape[0]
    for top in range(0, size, BLOCK):
        factor_block(work_ref, top)
        low = top + BLOCK
        if low < size:
            start = low // 128 * 128
            change = lax.dot_general(
                work_ref[top:low, start:size],
                work_ref[top:low, start:],
                (((0,), (0,)), ((), ())),
                precision=lax.Precision.HIGHEST,
                preferred_element_type=jnp.float32,
            )
            work_ref[low:, start:] = work_ref[low:, start:] - change[low - start :]


def tail_kernel(
    place_ref,
    sums_ref,
    other_ref,
    view_ref,
    scale_ref,
    columns_ref,
    target_ref,
    view_grad_ref,
    weight_grad_ref,
    work_ref,
    full_ref,
):
    samples, width = view_ref.shape
    share = target_ref.shape[0]
    block = sums_ref.shape[1] // 3
    half = samples // 2
    core = place_ref[1]

    def whole(part):
        lanes = slice(part * block, (part + 1) * block)
        mine = sums_ref[:, lanes, :].reshape(half, width)
        other = other_ref[:, lanes, :].reshape(half, width)
        return jnp.concatenate(
            [jnp.where(core == 0, mine, other), jnp.where(core == 0, other, mine)], axis=0
        )

    total = whole(0)
    mean = total * (1.0 / MODS)
    gram = lax.dot_general(
        mean, mean, (((0,), (0,)), ((), ())), preferred_element_type=jnp.float32
    )
    shape = (width, width)
    eye = lax.broadcasted_iota(jnp.int32, shape, 0) == lax.broadcasted_iota(jnp.int32, shape, 1)
    work_ref[:, :width] = gram / samples + jnp.where(eye, 0.001, 0.0)
    work_ref[:, width:] = jnp.where(eye, 1.0, 0.0)
    solve(work_ref)
    target = lax.dot_general(
        mean.astype(jnp.float32),
        work_ref[:, width:],
        (((1,), (1,)), ((), ())),
        precision=lax.Precision.HIGHEST,
        preferred_element_type=jnp.float32,
    )
    coupling = jnp.dot(whole(1), view_ref[:width, :], preferred_element_type=jnp.float32)
    coupling = coupling + jnp.dot(whole(2), view_ref[width:, :], preferred_element_type=jnp.float32)
    coupling = coupling / samples - total.astype(jnp.float32)
    view = view_ref[...].astype(jnp.float32)
    grad = view - target + coupling
    share_rows = pl.ds(pl.multiple_of(place_ref[0] * share, share), share)
    full_ref[...] = target
    target_ref[...] = full_ref[share_rows, :]
    full_ref[...] = grad
    view_grad_ref[...] = full_ref[share_rows, :].astype(jnp.bfloat16)
    inner = jnp.mean(grad * view, axis=-1, keepdims=True)
    scale = jnp.concatenate([scale_ref[...]] * (width // 128), axis=1)
    raw_grad = ((grad - view * inner) * scale).astype(jnp.bfloat16)
    weight_grad_ref[...] = jnp.dot(
        columns_ref[...], raw_grad, preferred_element_type=jnp.float32
    )


def finish(place, sums, other, view, scale, columns, share):
    samples, width = view.shape
    vmem = pl.BlockSpec(memory_space=pltpu.VMEM)
    return pl.pallas_call(
        tail_kernel,
        out_shape=(
            jax.ShapeDtypeStruct((share, width), jnp.float32),
            jax.ShapeDtypeStruct((share, width), jnp.bfloat16),
            jax.ShapeDtypeStruct((columns.shape[0], width), jnp.float32),
        ),
        in_specs=[pl.BlockSpec(memory_space=pltpu.SMEM)] + [vmem] * 5,
        out_specs=(vmem,) * 3,
        scratch_shapes=[
            pltpu.VMEM((width, 2 * width), jnp.float32),
            pltpu.VMEM((samples, width), jnp.float32),
        ],
        compiler_params=pltpu.CompilerParams(vmem_limit_bytes=12 * 1024 * 1024),
        name="finish",
    )(place, sums, other, view, scale, columns)


def swap(x, axis, groups=None):
    return lax.all_to_all(x, axis, 0, 0, tiled=True, axis_index_groups=groups)


def on_device(images, conv_first, conv_second, project, whiten, valid_mask, scene_index):
    samples = images.shape[1]
    size = lax.axis_size("sp")
    mods = lax.axis_size("mod")
    place = lax.axis_index("sp")
    share = samples // size
    rows = images.shape[2]
    x = images[0].reshape(size, share, rows, -1).transpose(0, 2, 1, 3)
    valid = valid_mask[0].reshape(size, share, 2, 4).transpose(0, 3, 2, 1)
    valid = valid.reshape(size, 4, 2 * share).astype(jnp.bfloat16)
    valid = jnp.pad(valid, ((0, 0), (0, EXTRA - 4), (0, 256 - 2 * share)))
    sent = jnp.concatenate([x.reshape(size, rows * share, -1), valid], axis=1)
    got = swap(sent, "sp")
    pooled = encode(got, conv_first[0], conv_second[0], share)
    pooled = swap(pooled, "sp").reshape(samples, CH)

    spot = jnp.stack([place, lax.axis_index("mod") % 2])
    columns, view, scale = make_view(
        spot, pooled, project[0], whiten[0], scene_index.reshape(1, samples), size
    )
    partner = [(i, i ^ 1) for i in range(mods)]
    chips = [[2 * i + core for i in range(mods // 2)] for core in range(2)]
    pieces = pair_sums(spot, view, lax.ppermute(view, "mod", partner), mods // 2)
    pieces = sum_spread(swap(pieces, "mod", chips))
    sums = swap(pieces, "mod", chips)
    other = lax.ppermute(sums, "mod", partner)
    target_rows, view_grad, grad_w = finish(spot, sums, other, view, scale, columns, share)
    return (target_rows, view_grad[None], grad_w[None])


def solution(mesh):
    placed = (
        P("mod", None, "sp", None),
        P("mod", None, None),
        P("mod", None, None),
        P("mod", None, None),
        P("mod", None, None),
        P("mod", None, "sp", None),
        P(),
    )
    return jax.shard_map(
        on_device,
        mesh=mesh,
        in_specs=placed,
        out_specs=(P("sp", None), P("mod", "sp", None), P("mod", "sp", None)),
        check_vma=False,
    )
```

```python
import jax
import jax.numpy as jnp
from jax import lax
from jax.experimental import pallas as pl
from jax.experimental.pallas import tpu as pltpu
from jax.sharding import PartitionSpec as P

BANDS = 16
CH = 256
SCENES = 64
MODS = 16
EXTRA = 8
TILE = 8
BLOCK = 64


def conv_kernel(got_ref, w1_ref, w2_ref, out_ref, padded_ref, band_ref, first_ref):
    sources = got_ref.shape[0]
    share = out_ref.shape[1]
    rows = (got_ref.shape[1] - EXTRA) // share
    window = 4 * BANDS
    groups = ((0, (0, 1, 2)), (64, (3, 4)), (128, (5, 6, 7)))
    band_ref[...] = jnp.zeros_like(band_ref)
    for start, columns in groups:
        for column in columns:
            low = 2 * BANDS * column - BANDS
            begin, end = (max(low, 0), min(low + window, 256))
            for tap in range(4):
                band_ref[
                    tap * 128 + begin - start : tap * 128 + end - start,
                    column * CH : (column + 1) * CH,
                ] = w1_ref[tap * window + begin - low : tap * window + end - low, :]

    total_rows = sources * rows
    blank = jnp.zeros((share, 256), jnp.bfloat16)
    padded_ref[0, 0] = blank
    padded_ref[total_rows // 2, 1] = blank
    for source in range(sources):
        for row in range(rows):
            place = source * rows + row + 1
            padded_ref[place // 2, place % 2] = got_ref[source, row * share : (row + 1) * share, :]
    blank = jnp.zeros((share, 8 * CH), jnp.bfloat16)
    first_ref[0, 0] = blank
    first_ref[total_rows // 4, 1] = blank

    step = 16

    def first_rows(group, carry):
        for start, columns in groups:
            left = jnp.concatenate(
                [
                    padded_ref[
                        pl.ds(group * step + tap // 2, step), tap % 2, :, start : start + 128
                    ].reshape(step * share, 128)
                    for tap in range(4)
                ],
                axis=1,
            )
            lanes = slice(columns[0] * CH, (columns[-1] + 1) * CH)
            total = jnp.dot(left, band_ref[:, lanes], preferred_element_type=jnp.float32)
            total = jnp.maximum(total, 0.0).astype(jnp.bfloat16)
            for row in range(step):
                first_ref[group * (step // 2) + (row + 1) // 2, (row + 1) % 2, :, lanes] = total[
                    row * share : (row + 1) * share
                ]
        return carry

    lax.fori_loop(0, total_rows // 2 // step, first_rows, 0)

    chunk = total_rows // 4
    span = chunk * share
    spot = lax.broadcasted_iota(jnp.int32, (share, span), 1) % share
    mine = spot == lax.broadcasted_iota(jnp.int32, (share, span), 0)
    pooled = jnp.zeros((share, CH), jnp.float32)
    for group in range(total_rows // 4 // chunk):
        for column in range(4):
            low, high = (max(2 * column - 1, 0), min(2 * column + 3, 8))
            skip = low - (2 * column - 1)
            total = None
            for tap in range(4):
                left = first_ref[
                    group * chunk + tap // 2 : group * chunk + tap // 2 + chunk,
                    tap % 2,
                    :,
                    low * CH : high * CH,
                ]
                part = jnp.dot(
                    left.reshape(span, (high - low) * CH),
                    w2_ref[(tap * 4 + skip) * CH : (tap * 4 + skip + high - low) * CH, :],
                    preferred_element_type=jnp.float32,
                )
                total = part if total is None else total + part
            pixel = jnp.maximum(total, 0.0).astype(jnp.bfloat16)
            row = rows * share + column
            valid = jnp.concatenate(
                [
                    got_ref[group * chunk // 2 + source, row : row + 1, : 2 * share].astype(jnp.float32)
                    for source in range(chunk // 2)
                ],
                axis=1,
            )
            chosen = jnp.where(mine, valid, 0.0).astype(jnp.bfloat16)
            pooled = pooled + jnp.dot(chosen, pixel, preferred_element_type=jnp.float32)
    cells = total_rows // 4 * 4
    pooled = (pooled / cells).astype(jnp.bfloat16)
    for source in range(sources):
        out_ref[source] = pooled


def encode(got, w1, w2, share):
    rows = got.shape[0] * (got.shape[1] - EXTRA) // share
    vmem = pl.BlockSpec(memory_space=pltpu.VMEM)
    return pl.pallas_call(
        conv_kernel,
        out_shape=jax.ShapeDtypeStruct((got.shape[0], share, CH), jnp.bfloat16),
        in_specs=[vmem] * 3,
        out_specs=vmem,
        scratch_shapes=[
            pltpu.VMEM((rows // 2 + 1, 2, share, 256), jnp.bfloat16),
            pltpu.VMEM((512, 8 * CH), jnp.bfloat16),
            pltpu.VMEM((rows // 4 + 1, 2, share, 8 * CH), jnp.bfloat16),
        ],
        compiler_params=pltpu.CompilerParams(vmem_limit_bytes=24 * 1024 * 1024),
        name="encode",
    )(got, w1, w2)


def chosen_sums(onehot, values, over):
    total = None
    for _ in range(3):
        part = values.astype(jnp.bfloat16)
        values = values - part.astype(jnp.float32)
        product = lax.dot_general(
            onehot, part, (((over,), (0,)), ((), ())), preferred_element_type=jnp.float32
        )
        total = product if total is None else total + product
    return total


def view_kernel(
    place_ref, pooled_ref, project_ref, whiten_ref, scene_ref, columns_ref, view_ref, scale_ref
):
    samples = pooled_ref.shape[0]
    feat = jnp.dot(pooled_ref[...], project_ref[...], preferred_element_type=jnp.float32)
    scene = lax.broadcasted_iota(jnp.int32, (SCENES, samples), 0)
    onehot = jnp.where(scene == scene_ref[...], 1.0, 0.0)
    counts = jnp.sum(onehot, axis=1, keepdims=True)
    half_onehot = onehot.astype(jnp.bfloat16)
    sums = chosen_sums(half_onehot, feat, 1)
    means = sums / jnp.maximum(counts, 1.0)
    own = chosen_sums(half_onehot, means, 0)
    panel = (feat - own).astype(jnp.bfloat16)
    raw = jnp.dot(panel, whiten_ref[...], preferred_element_type=jnp.float32)
    scale = lax.rsqrt(jnp.mean(raw * raw, axis=-1, keepdims=True) + 1e-05)
    scale_ref[...] = jnp.broadcast_to(scale, scale_ref.shape)
    view_ref[...] = (raw * scale).astype(jnp.bfloat16)
    wide, depth = (columns_ref.shape[0], panel.shape[1])
    feature = lax.broadcasted_iota(jnp.int32, (wide, depth), 1)
    wanted = lax.broadcasted_iota(jnp.int32, (wide, depth), 0) + place_ref[0] * wide
    pick = jnp.where(feature == wanted, 1.0, 0.0).astype(jnp.bfloat16)
    columns = lax.dot_general(
        pick, panel, (((1,), (1,)), ((), ())), preferred_element_type=jnp.float32
    )
    columns_ref[...] = columns.astype(jnp.bfloat16)


def make_view(place, pooled, project, whiten, scene, size):
    samples = pooled.shape[0]
    vmem = pl.BlockSpec(memory_space=pltpu.VMEM)
    return pl.pallas_call(
        view_kernel,
        out_shape=(
            jax.ShapeDtypeStruct((whiten.shape[0] // size, samples), jnp.bfloat16),
            jax.ShapeDtypeStruct((samples, CH), jnp.bfloat16),
            jax.ShapeDtypeStruct((samples, 128), jnp.float32),
        ),
        in_specs=[pl.BlockSpec(memory_space=pltpu.SMEM)] + [vmem] * 4,
        out_specs=(vmem,) * 3,
        compiler_params=pltpu.CompilerParams(vmem_limit_bytes=12 * 1024 * 1024),
        name="view",
    )(place, pooled, project, whiten, scene)


def pair_kernel(place_ref, view_ref, other_ref, out_ref):
    chips = out_ref.shape[0]
    half = view_ref.shape[0] // 2
    block = half // chips
    rows = pl.ds(pl.multiple_of(place_ref[1] * half, half), half)
    first, second = (view_ref[rows, :], other_ref[rows, :])
    both = first.astype(jnp.float32) + second.astype(jnp.float32)
    out_ref[:, :block, :] = both.astype(jnp.bfloat16).reshape(chips, block, CH)
    over = (((1,), (1,)), ((), ()))
    inner = lax.dot_general(first, view_ref[...], over, preferred_element_type=jnp.float32)
    inner = inner + lax.dot_general(
        second, other_ref[...], over, preferred_element_type=jnp.float32
    )
    inner = inner.astype(jnp.bfloat16)
    out_ref[:, block : 2 * block, :] = inner[:, :CH].reshape(chips, block, CH)
    out_ref[:, 2 * block :, :] = inner[:, CH:].reshape(chips, block, CH)


def pair_sums(place, view, other, chips):
    vmem = pl.BlockSpec(memory_space=pltpu.VMEM)
    block = view.shape[0] // 2 // chips
    return pl.pallas_call(
        pair_kernel,
        out_shape=jax.ShapeDtypeStruct((chips, 3 * block, CH), jnp.bfloat16),
        in_specs=[pl.BlockSpec(memory_space=pltpu.SMEM), vmem, vmem],
        out_specs=vmem,
        compiler_params=pltpu.CompilerParams(vmem_limit_bytes=8 * 1024 * 1024),
        name="pair",
    )(place, view, other)


def sum_kernel(in_ref, out_ref):
    total = in_ref[0].astype(jnp.float32)
    for source in range(1, in_ref.shape[0]):
        total = total + in_ref[source].astype(jnp.float32)
    total = total.astype(jnp.bfloat16)
    for source in range(in_ref.shape[0]):
        out_ref[source] = total


def sum_spread(x):
    vmem = pl.BlockSpec(memory_space=pltpu.VMEM)
    return pl.pallas_call(
        sum_kernel,
        out_shape=jax.ShapeDtypeStruct(x.shape, x.dtype),
        in_specs=[vmem],
        out_specs=vmem,
        compiler_params=pltpu.CompilerParams(vmem_limit_bytes=6 * 1024 * 1024),
        name="sums",
    )(x)


def pivot_inverse(columns):
    low = {}
    for j in range(TILE):
        for i in range(j, TILE):
            low[i, j] = jnp.broadcast_to(columns[j][i : i + 1, :], (TILE, 128))
    inverse = {}
    for j in range(TILE):
        root = lax.rsqrt(low[j, j])
        inverse[j, j] = root
        for i in range(j + 1, TILE):
            low[i, j] = low[i, j] * root
        for m in range(j + 1, TILE):
            for i in range(m, TILE):
                low[i, m] = low[i, m] - low[i, j] * low[m, j]
        for m in range(j):
            total = low[j, m] * inverse[m, m]
            for p in range(m + 1, j):
                total = total + low[j, p] * inverse[p, m]
            inverse[j, m] = -root * total
    return inverse


def factor_block(work_ref, top):
    half = work_ref.shape[1] // 256
    tiles = [t for t in range(top // 128, 2 * half) if t < half or (t - half) * 128 <= top]
    groups = BLOCK // TILE
    sub = lax.broadcasted_iota(jnp.int32, (TILE, 128), 0)
    rows = {}
    for g in range(groups):
        for t in tiles:
            rows[g, t] = work_ref[
                top + g * TILE : top + (g + 1) * TILE, t * 128 : (t + 1) * 128
            ]

    def lanes(g, tile, lane):
        return [
            jnp.broadcast_to(rows[g, tile][:, lane + j : lane + j + 1], (TILE, 128))
            for j in range(TILE)
        ]

    for g in range(groups):
        at = top + g * TILE
        tile, lane = (at // 128, at % 128)
        inverse = pivot_inverse(lanes(g, tile, lane))
        done = {}
        for j in range(TILE):
            column = inverse[TILE - 1, j]
            for i in range(TILE - 2, j - 1, -1):
                column = jnp.where(sub == i, inverse[i, j], column)
            if j:
                column = jnp.where(sub < j, 0.0, column)
            for t in tiles:
                part = column * jnp.broadcast_to(rows[g, t][j : j + 1, :], (TILE, 128))
                done[t] = part if j == 0 else done[t] + part
        for t in done:
            work_ref[at : at + TILE, t * 128 : (t + 1) * 128] = done[t]
        spreads = {
            (j, t): jnp.broadcast_to(done[t][j : j + 1, :], (TILE, 128))
            for t in done
            for j in range(TILE)
        }
        for h in range(g + 1, groups):
            columns = lanes(h, tile, lane)
            for j in range(TILE):
                weight = columns[0] * inverse[j, 0]
                for m in range(1, j + 1):
                    weight = weight + columns[m] * inverse[j, m]
                for t in done:
                    rows[h, t] = rows[h, t] - weight * spreads[j, t]


def solve(work_ref):
    size = work_ref.shape[0]
    for top in range(0, size, BLOCK):
        factor_block(work_ref, top)
        low = top + BLOCK
        if low < size:
            start = low // 128 * 128
            change = lax.dot_general(
                work_ref[top:low, start:size],
                work_ref[top:low, start:],
                (((0,), (0,)), ((), ())),
                precision=lax.Precision.HIGHEST,
                preferred_element_type=jnp.float32,
            )
            work_ref[low:, start:] = work_ref[low:, start:] - change[low - start :]


def tail_kernel(
    place_ref,
    sums_ref,
    other_ref,
    view_ref,
    scale_ref,
    columns_ref,
    target_ref,
    view_grad_ref,
    weight_grad_ref,
    work_ref,
    full_ref,
):
    samples, width = view_ref.shape
    share = target_ref.shape[0]
    block = sums_ref.shape[1] // 3
    half = samples // 2
    core = place_ref[1]

    def whole(part):
        lanes = slice(part * block, (part + 1) * block)
        mine = sums_ref[:, lanes, :].reshape(half, width)
        other = other_ref[:, lanes, :].reshape(half, width)
        return jnp.concatenate(
            [jnp.where(core == 0, mine, other), jnp.where(core == 0, other, mine)], axis=0
        )

    total = whole(0)
    mean = total * (1.0 / MODS)
    gram = lax.dot_general(
        mean, mean, (((0,), (0,)), ((), ())), preferred_element_type=jnp.float32
    )
    shape = (width, width)
    eye = lax.broadcasted_iota(jnp.int32, shape, 0) == lax.broadcasted_iota(jnp.int32, shape, 1)
    work_ref[:, :width] = gram / samples + jnp.where(eye, 0.001, 0.0)
    work_ref[:, width:] = jnp.where(eye, 1.0, 0.0)
    solve(work_ref)
    target = lax.dot_general(
        mean.astype(jnp.float32),
        work_ref[:, width:],
        (((1,), (1,)), ((), ())),
        precision=lax.Precision.HIGHEST,
        preferred_element_type=jnp.float32,
    )
    coupling = jnp.dot(whole(1), view_ref[:width, :], preferred_element_type=jnp.float32)
    coupling = coupling + jnp.dot(whole(2), view_ref[width:, :], preferred_element_type=jnp.float32)
    coupling = coupling / samples - total.astype(jnp.float32)
    view = view_ref[...].astype(jnp.float32)
    grad = view - target + coupling
    share_rows = pl.ds(pl.multiple_of(place_ref[0] * share, share), share)
    full_ref[...] = target
    target_ref[...] = full_ref[share_rows, :]
    full_ref[...] = grad
    view_grad_ref[...] = full_ref[share_rows, :].astype(jnp.bfloat16)
    inner = jnp.mean(grad * view, axis=-1, keepdims=True)
    scale = jnp.concatenate([scale_ref[...]] * (width // 128), axis=1)
    raw_grad = ((grad - view * inner) * scale).astype(jnp.bfloat16)
    weight_grad_ref[...] = jnp.dot(
        columns_ref[...], raw_grad, preferred_element_type=jnp.float32
    )


def finish(place, sums, other, view, scale, columns, share):
    samples, width = view.shape
    vmem = pl.BlockSpec(memory_space=pltpu.VMEM)
    return pl.pallas_call(
        tail_kernel,
        out_shape=(
            jax.ShapeDtypeStruct((share, width), jnp.float32),
            jax.ShapeDtypeStruct((share, width), jnp.bfloat16),
            jax.ShapeDtypeStruct((columns.shape[0], width), jnp.float32),
        ),
        in_specs=[pl.BlockSpec(memory_space=pltpu.SMEM)] + [vmem] * 5,
        out_specs=(vmem,) * 3,
        scratch_shapes=[
            pltpu.VMEM((width, 2 * width), jnp.float32),
            pltpu.VMEM((samples, width), jnp.float32),
        ],
        compiler_params=pltpu.CompilerParams(vmem_limit_bytes=12 * 1024 * 1024),
        name="finish",
    )(place, sums, other, view, scale, columns)


def swap(x, axis, groups=None):
    return lax.all_to_all(x, axis, 0, 0, tiled=True, axis_index_groups=groups)


def on_device(images, conv_first, conv_second, project, whiten, valid_mask, scene_index):
    samples = images.shape[1]
    size = lax.axis_size("sp")
    mods = lax.axis_size("mod")
    place = lax.axis_index("sp")
    share = samples // size
    rows = images.shape[2]
    x = images[0].reshape(size, share, rows, -1).transpose(0, 2, 1, 3)
    valid = valid_mask[0].reshape(size, share, 2, 4).transpose(0, 3, 2, 1)
    valid = valid.reshape(size, 4, 2 * share).astype(jnp.bfloat16)
    valid = jnp.pad(valid, ((0, 0), (0, EXTRA - 4), (0, 256 - 2 * share)))
    sent = jnp.concatenate([x.reshape(size, rows * share, -1), valid], axis=1)
    got = swap(sent, "sp")
    pooled = encode(got, conv_first[0], conv_second[0], share)
    pooled = swap(pooled, "sp").reshape(samples, CH)

    spot = jnp.stack([place, lax.axis_index("mod") % 2])
    columns, view, scale = make_view(
        spot, pooled, project[0], whiten[0], scene_index.reshape(1, samples), size
    )
    partner = [(i, i ^ 1) for i in range(mods)]
    chips = [[2 * i + core for i in range(mods // 2)] for core in range(2)]
    pieces = pair_sums(spot, view, lax.ppermute(view, "mod", partner), mods // 2)
    pieces = sum_spread(swap(pieces, "mod", chips))
    sums = swap(pieces, "mod", chips)
    other = lax.ppermute(sums, "mod", partner)
    target_rows, view_grad, grad_w = finish(spot, sums, other, view, scale, columns, share)
    return (target_rows, view_grad[None], grad_w[None])


def solution(mesh):
    placed = (
        P("mod", None, "sp", None),
        P("mod", None, None),
        P("mod", None, None),
        P("mod", None, None),
        P("mod", None, None),
        P("mod", None, "sp", None),
        P(),
    )
    return jax.shard_map(
        on_device,
        mesh=mesh,
        in_specs=placed,
        out_specs=(P("sp", None), P("mod", "sp", None), P("mod", "sp", None)),
        check_vma=False,
    )
```

```python
import jax
import jax.numpy as jnp
from jax import lax
from jax.experimental import pallas as pl
from jax.experimental.pallas import tpu as pltpu
from jax.sharding import PartitionSpec as P

BANDS = 16
CH = 256
SCENES = 64
MODS = 16
EXTRA = 8
TILE = 8
BLOCK = 64


def conv_kernel(got_ref, w1_ref, w2_ref, out_ref, padded_ref, band_ref, first_ref):
    sources = got_ref.shape[0]
    share = out_ref.shape[1]
    rows = (got_ref.shape[1] - EXTRA) // share
    window = 4 * BANDS
    groups = ((0, (0, 1, 2)), (64, (3, 4)), (128, (5, 6, 7)))
    band_ref[...] = jnp.zeros_like(band_ref)
    for start, columns in groups:
        for column in columns:
            low = 2 * BANDS * column - BANDS
            begin, end = (max(low, 0), min(low + window, 256))
            for tap in range(4):
                band_ref[
                    tap * 128 + begin - start : tap * 128 + end - start,
                    column * CH : (column + 1) * CH,
                ] = w1_ref[tap * window + begin - low : tap * window + end - low, :]

    total_rows = sources * rows
    blank = jnp.zeros((share, 256), jnp.bfloat16)
    padded_ref[0, 0] = blank
    padded_ref[total_rows // 2, 1] = blank
    for source in range(sources):
        for row in range(rows):
            place = source * rows + row + 1
            padded_ref[place // 2, place % 2] = got_ref[source, row * share : (row + 1) * share, :]
    blank = jnp.zeros((share, 8 * CH), jnp.bfloat16)
    first_ref[0, 0] = blank
    first_ref[total_rows // 4, 1] = blank

    step = 16

    def first_rows(group, carry):
        for start, columns in groups:
            left = jnp.concatenate(
                [
                    padded_ref[
                        pl.ds(group * step + tap // 2, step), tap % 2, :, start : start + 128
                    ].reshape(step * share, 128)
                    for tap in range(4)
                ],
                axis=1,
            )
            lanes = slice(columns[0] * CH, (columns[-1] + 1) * CH)
            total = jnp.dot(left, band_ref[:, lanes], preferred_element_type=jnp.float32)
            total = jnp.maximum(total, 0.0).astype(jnp.bfloat16)
            for row in range(step):
                first_ref[group * (step // 2) + (row + 1) // 2, (row + 1) % 2, :, lanes] = total[
                    row * share : (row + 1) * share
                ]
        return carry

    lax.fori_loop(0, total_rows // 2 // step, first_rows, 0)

    chunk = total_rows // 4
    span = chunk * share
    spot = lax.broadcasted_iota(jnp.int32, (share, span), 1) % share
    mine = spot == lax.broadcasted_iota(jnp.int32, (share, span), 0)
    pooled = jnp.zeros((share, CH), jnp.float32)
    for group in range(total_rows // 4 // chunk):
        for columns in ((0, 3), (1, 2)):
            totals = {}
            for tap in range(4):
                for column in columns:
                    low, high = (max(2 * column - 1, 0), min(2 * column + 3, 8))
                    skip = low - (2 * column - 1)
                    left = first_ref[
                        group * chunk + tap // 2 : group * chunk + tap // 2 + chunk,
                        tap % 2,
                        :,
                        low * CH : high * CH,
                    ]
                    part = jnp.dot(
                        left.reshape(span, (high - low) * CH),
                        w2_ref[(tap * 4 + skip) * CH : (tap * 4 + skip + high - low) * CH, :],
                        preferred_element_type=jnp.float32,
                    )
                    totals[column] = totals[column] + part if tap else part
            for column in columns:
                pixel = jnp.maximum(totals[column], 0.0).astype(jnp.bfloat16)
                row = rows * share + column
                valid = jnp.concatenate(
                    [
                        got_ref[
                            group * chunk // 2 + source, row : row + 1, : 2 * share
                        ].astype(jnp.float32)
                        for source in range(chunk // 2)
                    ],
                    axis=1,
                )
                chosen = jnp.where(mine, valid, 0.0).astype(jnp.bfloat16)
                pooled = pooled + jnp.dot(chosen, pixel, preferred_element_type=jnp.float32)
    cells = total_rows // 4 * 4
    pooled = (pooled / cells).astype(jnp.bfloat16)
    for source in range(sources):
        out_ref[source] = pooled


def encode(got, w1, w2, share):
    rows = got.shape[0] * (got.shape[1] - EXTRA) // share
    vmem = pl.BlockSpec(memory_space=pltpu.VMEM)
    return pl.pallas_call(
        conv_kernel,
        out_shape=jax.ShapeDtypeStruct((got.shape[0], share, CH), jnp.bfloat16),
        in_specs=[vmem] * 3,
        out_specs=vmem,
        scratch_shapes=[
            pltpu.VMEM((rows // 2 + 1, 2, share, 256), jnp.bfloat16),
            pltpu.VMEM((512, 8 * CH), jnp.bfloat16),
            pltpu.VMEM((rows // 4 + 1, 2, share, 8 * CH), jnp.bfloat16),
        ],
        compiler_params=pltpu.CompilerParams(vmem_limit_bytes=24 * 1024 * 1024),
        name="encode",
    )(got, w1, w2)


def chosen_sums(left, values, over, other=0):
    total = None
    for _ in range(3):
        part = values.astype(jnp.bfloat16)
        values = values - part.astype(jnp.float32)
        product = lax.dot_general(
            left, part, (((over,), (other,)), ((), ())), preferred_element_type=jnp.float32
        )
        total = product if total is None else total + product
    return total


def view_kernel(
    place_ref, pooled_ref, project_ref, whiten_ref, scene_ref, columns_ref, view_ref, scale_ref
):
    samples = pooled_ref.shape[0]
    feat = jnp.dot(pooled_ref[...], project_ref[...], preferred_element_type=jnp.float32)
    scene = lax.broadcasted_iota(jnp.int32, (SCENES, samples), 0)
    onehot = jnp.where(scene == scene_ref[...], 1.0, 0.0)
    counts = jnp.sum(onehot, axis=1, keepdims=True)
    half_onehot = onehot.astype(jnp.bfloat16)
    sums = chosen_sums(half_onehot, feat, 1)
    means = sums / jnp.maximum(counts, 1.0)
    own = chosen_sums(half_onehot, means, 0)
    panel = (feat - own).astype(jnp.bfloat16)
    raw = jnp.dot(panel, whiten_ref[...], preferred_element_type=jnp.float32)
    scale = lax.rsqrt(jnp.mean(raw * raw, axis=-1, keepdims=True) + 1e-05)
    scale_ref[...] = jnp.broadcast_to(scale, scale_ref.shape)
    view_ref[...] = (raw * scale).astype(jnp.bfloat16)
    wide, depth = (columns_ref.shape[0], panel.shape[1])
    feature = lax.broadcasted_iota(jnp.int32, (wide, depth), 1)
    wanted = lax.broadcasted_iota(jnp.int32, (wide, depth), 0) + place_ref[0] * wide
    pick = jnp.where(feature == wanted, 1.0, 0.0).astype(jnp.bfloat16)
    columns = lax.dot_general(
        pick, panel, (((1,), (1,)), ((), ())), preferred_element_type=jnp.float32
    )
    columns_ref[...] = columns.astype(jnp.bfloat16)


def make_view(place, pooled, project, whiten, scene, size):
    samples = pooled.shape[0]
    vmem = pl.BlockSpec(memory_space=pltpu.VMEM)
    return pl.pallas_call(
        view_kernel,
        out_shape=(
            jax.ShapeDtypeStruct((whiten.shape[0] // size, samples), jnp.bfloat16),
            jax.ShapeDtypeStruct((samples, CH), jnp.bfloat16),
            jax.ShapeDtypeStruct((samples, 128), jnp.float32),
        ),
        in_specs=[pl.BlockSpec(memory_space=pltpu.SMEM)] + [vmem] * 4,
        out_specs=(vmem,) * 3,
        compiler_params=pltpu.CompilerParams(vmem_limit_bytes=12 * 1024 * 1024),
        name="view",
    )(place, pooled, project, whiten, scene)


def pair_kernel(place_ref, view_ref, other_ref, out_ref):
    chips = out_ref.shape[0]
    half = view_ref.shape[0] // 2
    block = half // chips
    rows = pl.ds(pl.multiple_of(place_ref[1] * half, half), half)
    first, second = (view_ref[rows, :], other_ref[rows, :])
    both = first.astype(jnp.float32) + second.astype(jnp.float32)
    out_ref[:, :block, :] = both.astype(jnp.bfloat16).reshape(chips, block, CH)
    over = (((1,), (1,)), ((), ()))
    inner = lax.dot_general(first, view_ref[...], over, preferred_element_type=jnp.float32)
    inner = inner + lax.dot_general(
        second, other_ref[...], over, preferred_element_type=jnp.float32
    )
    inner = inner.astype(jnp.bfloat16)
    out_ref[:, block : 2 * block, :] = inner[:, :CH].reshape(chips, block, CH)
    out_ref[:, 2 * block :, :] = inner[:, CH:].reshape(chips, block, CH)


def pair_sums(place, view, other, chips):
    vmem = pl.BlockSpec(memory_space=pltpu.VMEM)
    block = view.shape[0] // 2 // chips
    return pl.pallas_call(
        pair_kernel,
        out_shape=jax.ShapeDtypeStruct((chips, 3 * block, CH), jnp.bfloat16),
        in_specs=[pl.BlockSpec(memory_space=pltpu.SMEM), vmem, vmem],
        out_specs=vmem,
        compiler_params=pltpu.CompilerParams(vmem_limit_bytes=8 * 1024 * 1024),
        name="pair",
    )(place, view, other)


def sum_kernel(in_ref, out_ref):
    total = in_ref[0].astype(jnp.float32)
    for source in range(1, in_ref.shape[0]):
        total = total + in_ref[source].astype(jnp.float32)
    total = total.astype(jnp.bfloat16)
    for source in range(in_ref.shape[0]):
        out_ref[source] = total


def sum_spread(x):
    vmem = pl.BlockSpec(memory_space=pltpu.VMEM)
    return pl.pallas_call(
        sum_kernel,
        out_shape=jax.ShapeDtypeStruct(x.shape, x.dtype),
        in_specs=[vmem],
        out_specs=vmem,
        compiler_params=pltpu.CompilerParams(vmem_limit_bytes=6 * 1024 * 1024),
        name="sums",
    )(x)


def pivot_inverse(columns):
    low = {}
    for j in range(TILE):
        for i in range(j, TILE):
            low[i, j] = jnp.broadcast_to(columns[j][i : i + 1, :], (TILE, 128))
    inverse = {}
    for j in range(TILE):
        root = lax.rsqrt(low[j, j])
        inverse[j, j] = root
        for i in range(j + 1, TILE):
            low[i, j] = low[i, j] * root
        for m in range(j + 1, TILE):
            for i in range(m, TILE):
                low[i, m] = low[i, m] - low[i, j] * low[m, j]
        for m in range(j):
            total = low[j, m] * inverse[m, m]
            for p in range(m + 1, j):
                total = total + low[j, p] * inverse[p, m]
            inverse[j, m] = -root * total
    return inverse


def factor_block(work_ref, top):
    half = work_ref.shape[1] // 256
    tiles = [t for t in range(top // 128, 2 * half) if t < half or (t - half) * 128 <= top]
    groups = BLOCK // TILE
    sub = lax.broadcasted_iota(jnp.int32, (TILE, 128), 0)
    rows = {}
    for g in range(groups):
        for t in tiles:
            rows[g, t] = work_ref[
                top + g * TILE : top + (g + 1) * TILE, t * 128 : (t + 1) * 128
            ]

    def lanes(g, tile, lane):
        return [
            jnp.broadcast_to(rows[g, tile][:, lane + j : lane + j + 1], (TILE, 128))
            for j in range(TILE)
        ]

    for g in range(groups):
        at = top + g * TILE
        tile, lane = (at // 128, at % 128)
        inverse = pivot_inverse(lanes(g, tile, lane))
        done = {}
        for j in range(TILE):
            column = inverse[TILE - 1, j]
            for i in range(TILE - 2, j - 1, -1):
                column = jnp.where(sub == i, inverse[i, j], column)
            if j:
                column = jnp.where(sub < j, 0.0, column)
            for t in tiles:
                part = column * jnp.broadcast_to(rows[g, t][j : j + 1, :], (TILE, 128))
                done[t] = part if j == 0 else done[t] + part
        for t in done:
            work_ref[at : at + TILE, t * 128 : (t + 1) * 128] = done[t]
        spreads = {
            (j, t): jnp.broadcast_to(done[t][j : j + 1, :], (TILE, 128))
            for t in done
            for j in range(TILE)
        }
        for h in range(g + 1, groups):
            columns = lanes(h, tile, lane)
            for j in range(TILE):
                weight = columns[0] * inverse[j, 0]
                for m in range(1, j + 1):
                    weight = weight + columns[m] * inverse[j, m]
                for t in done:
                    rows[h, t] = rows[h, t] - weight * spreads[j, t]


def solve(work_ref, beside):
    size = work_ref.shape[0]
    for top in range(0, size, BLOCK):
        factor_block(work_ref, top)
        low = top + BLOCK
        if low < size:
            start = low // 128 * 128
            change = lax.dot_general(
                work_ref[top:low, start:size],
                work_ref[top:low, start:],
                (((0,), (0,)), ((), ())),
                precision=lax.Precision.HIGHEST,
                preferred_element_type=jnp.float32,
            )
            if beside:
                beside.pop(0)()
            work_ref[low:, start:] = work_ref[low:, start:] - change[low - start :]


def tail_kernel(
    place_ref,
    sums_ref,
    other_ref,
    view_ref,
    scale_ref,
    columns_ref,
    target_ref,
    view_grad_ref,
    weight_grad_ref,
    work_ref,
    full_ref,
):
    samples, width = view_ref.shape
    share = target_ref.shape[0]
    block = sums_ref.shape[1] // 3
    half = samples // 2
    core = place_ref[1]

    def whole(part):
        lanes = slice(part * block, (part + 1) * block)
        mine = sums_ref[:, lanes, :].reshape(half, width)
        other = other_ref[:, lanes, :].reshape(half, width)
        return jnp.concatenate(
            [jnp.where(core == 0, mine, other), jnp.where(core == 0, other, mine)], axis=0
        )

    total, left, right = (whole(0), whole(1), whole(2))
    mean = total * (1.0 / MODS)
    gram = lax.dot_general(
        mean, mean, (((0,), (0,)), ((), ())), preferred_element_type=jnp.float32
    )
    shape = (width, width)
    eye = lax.broadcasted_iota(jnp.int32, shape, 0) == lax.broadcasted_iota(jnp.int32, shape, 1)
    work_ref[:, :width] = gram / samples + jnp.where(eye, 0.001, 0.0)
    work_ref[:, width:] = jnp.where(eye, 1.0, 0.0)

    def couple(low):
        rows = slice(low, low + half)
        part = jnp.dot(left[rows], view_ref[:width, :], preferred_element_type=jnp.float32)
        full_ref[rows, :] = part + jnp.dot(
            right[rows], view_ref[width:, :], preferred_element_type=jnp.float32
        )

    solve(work_ref, [lambda: couple(0), lambda: couple(half)])
    target = chosen_sums(mean, work_ref[:, width:], 1, 1)
    coupling = full_ref[...]
    coupling = coupling / samples - total.astype(jnp.float32)
    view = view_ref[...].astype(jnp.float32)
    grad = view - target + coupling
    share_rows = pl.ds(pl.multiple_of(place_ref[0] * share, share), share)
    full_ref[...] = target
    target_ref[...] = full_ref[share_rows, :]
    full_ref[...] = grad
    view_grad_ref[...] = full_ref[share_rows, :].astype(jnp.bfloat16)
    inner = jnp.mean(grad * view, axis=-1, keepdims=True)
    scale = jnp.concatenate([scale_ref[...]] * (width // 128), axis=1)
    raw_grad = ((grad - view * inner) * scale).astype(jnp.bfloat16)
    weight_grad_ref[...] = jnp.dot(
        columns_ref[...], raw_grad, preferred_element_type=jnp.float32
    )


def finish(place, sums, other, view, scale, columns, share):
    samples, width = view.shape
    vmem = pl.BlockSpec(memory_space=pltpu.VMEM)
    return pl.pallas_call(
        tail_kernel,
        out_shape=(
            jax.ShapeDtypeStruct((share, width), jnp.float32),
            jax.ShapeDtypeStruct((share, width), jnp.bfloat16),
            jax.ShapeDtypeStruct((columns.shape[0], width), jnp.float32),
        ),
        in_specs=[pl.BlockSpec(memory_space=pltpu.SMEM)] + [vmem] * 5,
        out_specs=(vmem,) * 3,
        scratch_shapes=[
            pltpu.VMEM((width, 2 * width), jnp.float32),
            pltpu.VMEM((samples, width), jnp.float32),
        ],
        compiler_params=pltpu.CompilerParams(vmem_limit_bytes=12 * 1024 * 1024),
        name="finish",
    )(place, sums, other, view, scale, columns)


def swap(x, axis, groups=None):
    return lax.all_to_all(x, axis, 0, 0, tiled=True, axis_index_groups=groups)


def on_device(images, conv_first, conv_second, project, whiten, valid_mask, scene_index):
    samples = images.shape[1]
    size = lax.axis_size("sp")
    mods = lax.axis_size("mod")
    place = lax.axis_index("sp")
    share = samples // size
    rows = images.shape[2]
    x = images[0].reshape(size, share, rows, -1).transpose(0, 2, 1, 3)
    valid = valid_mask[0].reshape(size, share, 2, 4).transpose(0, 3, 2, 1)
    valid = valid.reshape(size, 4, 2 * share).astype(jnp.bfloat16)
    valid = jnp.pad(valid, ((0, 0), (0, EXTRA - 4), (0, 256 - 2 * share)))
    sent = jnp.concatenate([x.reshape(size, rows * share, -1), valid], axis=1)
    got = swap(sent, "sp")
    pooled = encode(got, conv_first[0], conv_second[0], share)
    pooled = swap(pooled, "sp").reshape(samples, CH)

    spot = jnp.stack([place, lax.axis_index("mod") % 2])
    columns, view, scale = make_view(
        spot, pooled, project[0], whiten[0], scene_index.reshape(1, samples), size
    )
    partner = [(i, i ^ 1) for i in range(mods)]
    chips = [[2 * i + core for i in range(mods // 2)] for core in range(2)]
    pieces = pair_sums(spot, view, lax.ppermute(view, "mod", partner), mods // 2)
    pieces = sum_spread(swap(pieces, "mod", chips))
    sums = swap(pieces, "mod", chips)
    other = lax.ppermute(sums, "mod", partner)
    target_rows, view_grad, grad_w = finish(spot, sums, other, view, scale, columns, share)
    return (target_rows, view_grad[None], grad_w[None])


def solution(mesh):
    placed = (
        P("mod", None, "sp", None),
        P("mod", None, None),
        P("mod", None, None),
        P("mod", None, None),
        P("mod", None, None),
        P("mod", None, "sp", None),
        P(),
    )
    return jax.shard_map(
        on_device,
        mesh=mesh,
        in_specs=placed,
        out_specs=(P("sp", None), P("mod", "sp", None), P("mod", "sp", None)),
        check_vma=False,
    )
```

```python
import jax
import jax.numpy as jnp
from jax import lax
from jax.experimental import pallas as pl
from jax.experimental.pallas import tpu as pltpu
from jax.sharding import PartitionSpec as P

BANDS = 16
CH = 256
SCENES = 64
MODS = 16
EXTRA = 8
TILE = 8
BLOCK = 64


def conv_kernel(got_ref, w1_ref, w2_ref, out_ref, padded_ref, band_ref, first_ref):
    sources = got_ref.shape[0]
    share = out_ref.shape[1]
    rows = (got_ref.shape[1] - EXTRA) // share
    window = 4 * BANDS
    groups = ((0, (0, 1, 2)), (64, (3, 4)), (128, (5, 6, 7)))
    band_ref[...] = jnp.zeros_like(band_ref)
    for start, columns in groups:
        for column in columns:
            low = 2 * BANDS * column - BANDS
            begin, end = (max(low, 0), min(low + window, 256))
            for tap in range(4):
                band_ref[
                    tap * 128 + begin - start : tap * 128 + end - start,
                    column * CH : (column + 1) * CH,
                ] = w1_ref[tap * window + begin - low : tap * window + end - low, :]

    total_rows = sources * rows
    blank = jnp.zeros((share, 256), jnp.bfloat16)
    padded_ref[0, 0] = blank
    padded_ref[total_rows // 2, 1] = blank
    for source in range(sources):
        for row in range(rows):
            place = source * rows + row + 1
            padded_ref[place // 2, place % 2] = got_ref[source, row * share : (row + 1) * share, :]
    blank = jnp.zeros((share, 8 * CH), jnp.bfloat16)
    first_ref[0, 0] = blank
    first_ref[total_rows // 4, 1] = blank

    step = 16

    def first_rows(group, carry):
        for start, columns in groups:
            left = jnp.concatenate(
                [
                    padded_ref[
                        pl.ds(group * step + tap // 2, step), tap % 2, :, start : start + 128
                    ].reshape(step * share, 128)
                    for tap in range(4)
                ],
                axis=1,
            )
            lanes = slice(columns[0] * CH, (columns[-1] + 1) * CH)
            total = jnp.dot(left, band_ref[:, lanes], preferred_element_type=jnp.float32)
            total = jnp.maximum(total, 0.0).astype(jnp.bfloat16)
            for row in range(step):
                first_ref[group * (step // 2) + (row + 1) // 2, (row + 1) % 2, :, lanes] = total[
                    row * share : (row + 1) * share
                ]
        return carry

    lax.fori_loop(0, total_rows // 2 // step, first_rows, 0)

    chunk = total_rows // 4
    span = chunk * share
    spot = lax.broadcasted_iota(jnp.int32, (share, span), 1) % share
    mine = spot == lax.broadcasted_iota(jnp.int32, (share, span), 0)
    pooled = jnp.zeros((share, CH), jnp.float32)
    for group in range(total_rows // 4 // chunk):
        for columns in ((0, 3), (1, 2)):
            totals = {}
            for tap in range(4):
                for column in columns:
                    low, high = (max(2 * column - 1, 0), min(2 * column + 3, 8))
                    skip = low - (2 * column - 1)
                    left = first_ref[
                        group * chunk + tap // 2 : group * chunk + tap // 2 + chunk,
                        tap % 2,
                        :,
                        low * CH : high * CH,
                    ]
                    part = jnp.dot(
                        left.reshape(span, (high - low) * CH),
                        w2_ref[(tap * 4 + skip) * CH : (tap * 4 + skip + high - low) * CH, :],
                        preferred_element_type=jnp.float32,
                    )
                    totals[column] = totals[column] + part if tap else part
            for column in columns:
                pixel = jnp.maximum(totals[column], 0.0).astype(jnp.bfloat16)
                row = rows * share + column
                valid = jnp.concatenate(
                    [
                        got_ref[
                            group * chunk // 2 + source, row : row + 1, : 2 * share
                        ].astype(jnp.float32)
                        for source in range(chunk // 2)
                    ],
                    axis=1,
                )
                chosen = jnp.where(mine, valid, 0.0).astype(jnp.bfloat16)
                pooled = pooled + jnp.dot(chosen, pixel, preferred_element_type=jnp.float32)
    cells = total_rows // 4 * 4
    pooled = (pooled / cells).astype(jnp.bfloat16)
    for source in range(sources):
        out_ref[source] = pooled


def encode(got, w1, w2, share):
    rows = got.shape[0] * (got.shape[1] - EXTRA) // share
    vmem = pl.BlockSpec(memory_space=pltpu.VMEM)
    return pl.pallas_call(
        conv_kernel,
        out_shape=jax.ShapeDtypeStruct((got.shape[0], share, CH), jnp.bfloat16),
        in_specs=[vmem] * 3,
        out_specs=vmem,
        scratch_shapes=[
            pltpu.VMEM((rows // 2 + 1, 2, share, 256), jnp.bfloat16),
            pltpu.VMEM((512, 8 * CH), jnp.bfloat16),
            pltpu.VMEM((rows // 4 + 1, 2, share, 8 * CH), jnp.bfloat16),
        ],
        compiler_params=pltpu.CompilerParams(vmem_limit_bytes=24 * 1024 * 1024),
        name="encode",
    )(got, w1, w2)


def chosen_sums(left, values, over, other=0):
    total = None
    for _ in range(3):
        part = values.astype(jnp.bfloat16)
        values = values - part.astype(jnp.float32)
        product = lax.dot_general(
            left, part, (((over,), (other,)), ((), ())), preferred_element_type=jnp.float32
        )
        total = product if total is None else total + product
    return total


def view_kernel(
    place_ref, pooled_ref, project_ref, whiten_ref, scene_ref, columns_ref, view_ref, scale_ref
):
    samples = pooled_ref.shape[0]
    feat = jnp.dot(pooled_ref[...], project_ref[...], preferred_element_type=jnp.float32)
    scene = lax.broadcasted_iota(jnp.int32, (SCENES, samples), 0)
    onehot = jnp.where(scene == scene_ref[...], 1.0, 0.0)
    counts = jnp.sum(onehot, axis=1, keepdims=True)
    half_onehot = onehot.astype(jnp.bfloat16)
    sums = chosen_sums(half_onehot, feat, 1)
    means = sums / jnp.maximum(counts, 1.0)
    own = chosen_sums(half_onehot, means, 0)
    panel = (feat - own).astype(jnp.bfloat16)
    raw = jnp.dot(panel, whiten_ref[...], preferred_element_type=jnp.float32)
    scale = lax.rsqrt(jnp.mean(raw * raw, axis=-1, keepdims=True) + 1e-05)
    scale_ref[...] = jnp.broadcast_to(scale, scale_ref.shape)
    view_ref[...] = (raw * scale).astype(jnp.bfloat16)
    wide, depth = (columns_ref.shape[0], panel.shape[1])
    feature = lax.broadcasted_iota(jnp.int32, (wide, depth), 1)
    wanted = lax.broadcasted_iota(jnp.int32, (wide, depth), 0) + place_ref[0] * wide
    pick = jnp.where(feature == wanted, 1.0, 0.0).astype(jnp.bfloat16)
    columns = lax.dot_general(
        pick, panel, (((1,), (1,)), ((), ())), preferred_element_type=jnp.float32
    )
    columns_ref[...] = columns.astype(jnp.bfloat16)


def make_view(place, pooled, project, whiten, scene, size):
    samples = pooled.shape[0]
    vmem = pl.BlockSpec(memory_space=pltpu.VMEM)
    return pl.pallas_call(
        view_kernel,
        out_shape=(
            jax.ShapeDtypeStruct((whiten.shape[0] // size, samples), jnp.bfloat16),
            jax.ShapeDtypeStruct((samples, CH), jnp.bfloat16),
            jax.ShapeDtypeStruct((samples, 128), jnp.float32),
        ),
        in_specs=[pl.BlockSpec(memory_space=pltpu.SMEM)] + [vmem] * 4,
        out_specs=(vmem,) * 3,
        compiler_params=pltpu.CompilerParams(vmem_limit_bytes=12 * 1024 * 1024),
        name="view",
    )(place, pooled, project, whiten, scene)


def pair_kernel(place_ref, view_ref, other_ref, out_ref):
    chips = out_ref.shape[0]
    half = view_ref.shape[0] // 2
    block = half // chips
    rows = pl.ds(pl.multiple_of(place_ref[1] * half, half), half)
    first, second = (view_ref[rows, :], other_ref[rows, :])
    both = first.astype(jnp.float32) + second.astype(jnp.float32)
    out_ref[:, :block, :] = both.astype(jnp.bfloat16).reshape(chips, block, CH)
    over = (((1,), (1,)), ((), ()))
    inner = lax.dot_general(first, view_ref[...], over, preferred_element_type=jnp.float32)
    inner = inner + lax.dot_general(
        second, other_ref[...], over, preferred_element_type=jnp.float32
    )
    inner = inner.astype(jnp.bfloat16)
    out_ref[:, block : 2 * block, :] = inner[:, :CH].reshape(chips, block, CH)
    out_ref[:, 2 * block :, :] = inner[:, CH:].reshape(chips, block, CH)


def pair_sums(place, view, other, chips):
    vmem = pl.BlockSpec(memory_space=pltpu.VMEM)
    block = view.shape[0] // 2 // chips
    return pl.pallas_call(
        pair_kernel,
        out_shape=jax.ShapeDtypeStruct((chips, 3 * block, CH), jnp.bfloat16),
        in_specs=[pl.BlockSpec(memory_space=pltpu.SMEM), vmem, vmem],
        out_specs=vmem,
        compiler_params=pltpu.CompilerParams(vmem_limit_bytes=8 * 1024 * 1024),
        name="pair",
    )(place, view, other)


def sum_kernel(in_ref, out_ref):
    total = in_ref[0].astype(jnp.float32)
    for source in range(1, in_ref.shape[0]):
        total = total + in_ref[source].astype(jnp.float32)
    total = total.astype(jnp.bfloat16)
    for source in range(in_ref.shape[0]):
        out_ref[source] = total


def sum_spread(x):
    vmem = pl.BlockSpec(memory_space=pltpu.VMEM)
    return pl.pallas_call(
        sum_kernel,
        out_shape=jax.ShapeDtypeStruct(x.shape, x.dtype),
        in_specs=[vmem],
        out_specs=vmem,
        compiler_params=pltpu.CompilerParams(vmem_limit_bytes=6 * 1024 * 1024),
        name="sums",
    )(x)


def pivot_inverse(columns):
    low = {}
    for j in range(TILE):
        for i in range(j, TILE):
            low[i, j] = jnp.broadcast_to(columns[j][i : i + 1, :], (TILE, 128))
    inverse = {}
    for j in range(TILE):
        root = lax.rsqrt(low[j, j])
        inverse[j, j] = root
        for i in range(j + 1, TILE):
            low[i, j] = low[i, j] * root
        for m in range(j + 1, TILE):
            for i in range(m, TILE):
                low[i, m] = low[i, m] - low[i, j] * low[m, j]
        for m in range(j):
            total = low[j, m] * inverse[m, m]
            for p in range(m + 1, j):
                total = total + low[j, p] * inverse[p, m]
            inverse[j, m] = -root * total
    return inverse


def factor_block(work_ref, top):
    half = work_ref.shape[1] // 256
    tiles = [t for t in range(top // 128, 2 * half) if t < half or (t - half) * 128 <= top]
    groups = BLOCK // TILE
    sub = lax.broadcasted_iota(jnp.int32, (TILE, 128), 0)
    rows = {}
    for g in range(groups):
        for t in tiles:
            rows[g, t] = work_ref[
                top + g * TILE : top + (g + 1) * TILE, t * 128 : (t + 1) * 128
            ]

    def lanes(g, tile, lane):
        return [
            jnp.broadcast_to(rows[g, tile][:, lane + j : lane + j + 1], (TILE, 128))
            for j in range(TILE)
        ]

    for g in range(groups):
        at = top + g * TILE
        tile, lane = (at // 128, at % 128)
        inverse = pivot_inverse(lanes(g, tile, lane))
        done = {}
        for j in range(TILE):
            column = inverse[TILE - 1, j]
            for i in range(TILE - 2, j - 1, -1):
                column = jnp.where(sub == i, inverse[i, j], column)
            if j:
                column = jnp.where(sub < j, 0.0, column)
            for t in tiles:
                part = column * jnp.broadcast_to(rows[g, t][j : j + 1, :], (TILE, 128))
                done[t] = part if j == 0 else done[t] + part
        for t in done:
            work_ref[at : at + TILE, t * 128 : (t + 1) * 128] = done[t]
        spreads = {
            (j, t): jnp.broadcast_to(done[t][j : j + 1, :], (TILE, 128))
            for t in done
            for j in range(TILE)
        }
        for h in range(g + 1, groups):
            columns = lanes(h, tile, lane)
            for j in range(TILE):
                weight = columns[0] * inverse[j, 0]
                for m in range(1, j + 1):
                    weight = weight + columns[m] * inverse[j, m]
                for t in done:
                    rows[h, t] = rows[h, t] - weight * spreads[j, t]


def solve(work_ref, beside):
    size = work_ref.shape[0]
    for top in range(0, size, BLOCK):
        factor_block(work_ref, top)
        low = top + BLOCK
        if low < size:
            start = low // 128 * 128
            change = lax.dot_general(
                work_ref[top:low, start:size],
                work_ref[top:low, start:],
                (((0,), (0,)), ((), ())),
                precision=lax.Precision.HIGHEST,
                preferred_element_type=jnp.float32,
            )
            if beside:
                beside.pop(0)()
            work_ref[low:, start:] = work_ref[low:, start:] - change[low - start :]


def tail_kernel(
    place_ref,
    sums_ref,
    other_ref,
    view_ref,
    scale_ref,
    columns_ref,
    target_ref,
    view_grad_ref,
    weight_grad_ref,
    work_ref,
    full_ref,
):
    samples, width = view_ref.shape
    share = target_ref.shape[0]
    block = sums_ref.shape[1] // 3
    half = samples // 2
    core = place_ref[1]

    def whole(part):
        lanes = slice(part * block, (part + 1) * block)
        mine = sums_ref[:, lanes, :].reshape(half, width)
        other = other_ref[:, lanes, :].reshape(half, width)
        return jnp.concatenate(
            [jnp.where(core == 0, mine, other), jnp.where(core == 0, other, mine)], axis=0
        )

    total, left, right = (whole(0), whole(1), whole(2))
    mean = total * (1.0 / MODS)
    gram = lax.dot_general(
        mean, mean, (((0,), (0,)), ((), ())), preferred_element_type=jnp.float32
    )
    shape = (width, width)
    eye = lax.broadcasted_iota(jnp.int32, shape, 0) == lax.broadcasted_iota(jnp.int32, shape, 1)
    work_ref[:, :width] = gram / samples + jnp.where(eye, 0.001, 0.0)
    work_ref[:, width:] = jnp.where(eye, 1.0, 0.0)

    def couple(low):
        rows = slice(low, low + half)
        part = jnp.dot(left[rows], view_ref[:width, :], preferred_element_type=jnp.float32)
        full_ref[rows, :] = part + jnp.dot(
            right[rows], view_ref[width:, :], preferred_element_type=jnp.float32
        )

    solve(work_ref, [lambda: couple(0), lambda: couple(half)])
    target = chosen_sums(mean, work_ref[:, width:], 1, 1)
    coupling = full_ref[...]
    coupling = coupling / samples - total.astype(jnp.float32)
    view = view_ref[...].astype(jnp.float32)
    grad = view - target + coupling
    share_rows = pl.ds(pl.multiple_of(place_ref[0] * share, share), share)
    full_ref[...] = target
    target_ref[...] = full_ref[share_rows, :]
    full_ref[...] = grad
    view_grad_ref[...] = full_ref[share_rows, :].astype(jnp.bfloat16)
    inner = jnp.mean(grad * view, axis=-1, keepdims=True)
    scale = jnp.concatenate([scale_ref[...]] * (width // 128), axis=1)
    raw_grad = ((grad - view * inner) * scale).astype(jnp.bfloat16)
    weight_grad_ref[...] = jnp.dot(
        columns_ref[...], raw_grad, preferred_element_type=jnp.float32
    )


def finish(place, sums, other, view, scale, columns, share):
    samples, width = view.shape
    vmem = pl.BlockSpec(memory_space=pltpu.VMEM)
    return pl.pallas_call(
        tail_kernel,
        out_shape=(
            jax.ShapeDtypeStruct((share, width), jnp.float32),
            jax.ShapeDtypeStruct((share, width), jnp.bfloat16),
            jax.ShapeDtypeStruct((columns.shape[0], width), jnp.float32),
        ),
        in_specs=[pl.BlockSpec(memory_space=pltpu.SMEM)] + [vmem] * 5,
        out_specs=(vmem,) * 3,
        scratch_shapes=[
            pltpu.VMEM((width, 2 * width), jnp.float32),
            pltpu.VMEM((samples, width), jnp.float32),
        ],
        compiler_params=pltpu.CompilerParams(vmem_limit_bytes=12 * 1024 * 1024),
        name="finish",
    )(place, sums, other, view, scale, columns)


def swap(x, axis, groups=None):
    return lax.all_to_all(x, axis, 0, 0, tiled=True, axis_index_groups=groups)


def on_device(images, conv_first, conv_second, project, whiten, valid_mask, scene_index):
    samples = images.shape[1]
    size = lax.axis_size("sp")
    mods = lax.axis_size("mod")
    place = lax.axis_index("sp")
    share = samples // size
    rows = images.shape[2]
    x = images[0].reshape(size, share, rows, -1).transpose(0, 2, 1, 3)
    x, valid = lax.optimization_barrier((x, valid_mask))
    valid = valid[0].reshape(size, share, 2, 4).transpose(0, 3, 2, 1)
    valid = valid.reshape(size, 4, 2 * share).astype(jnp.bfloat16)
    valid = jnp.pad(valid, ((0, 0), (0, EXTRA - 4), (0, 256 - 2 * share)))
    sent = jnp.concatenate([x.reshape(size, rows * share, -1), valid], axis=1)
    got = swap(sent, "sp")
    pooled = encode(got, conv_first[0], conv_second[0], share)
    pooled = swap(pooled, "sp").reshape(samples, CH)

    spot = jnp.stack([place, lax.axis_index("mod") % 2])
    columns, view, scale = make_view(
        spot, pooled, project[0], whiten[0], scene_index.reshape(1, samples), size
    )
    partner = [(i, i ^ 1) for i in range(mods)]
    chips = [[2 * i + core for i in range(mods // 2)] for core in range(2)]
    pieces = pair_sums(spot, view, lax.ppermute(view, "mod", partner), mods // 2)
    pieces = sum_spread(swap(pieces, "mod", chips))
    sums = swap(pieces, "mod", chips)
    other = lax.ppermute(sums, "mod", partner)
    target_rows, view_grad, grad_w = finish(spot, sums, other, view, scale, columns, share)
    return (target_rows, view_grad[None], grad_w[None])


def solution(mesh):
    placed = (
        P("mod", None, "sp", None),
        P("mod", None, None),
        P("mod", None, None),
        P("mod", None, None),
        P("mod", None, None),
        P("mod", None, "sp", None),
        P(),
    )
    return jax.shard_map(
        on_device,
        mesh=mesh,
        in_specs=placed,
        out_specs=(P("sp", None), P("mod", "sp", None), P("mod", "sp", None)),
        check_vma=False,
    )
```
